32 devices in a mesh: tp: 4 (over y, core), fsdp: 8 (over z, x).
Axes of the slice: x: 2, y: 2, z: 4, core: 2. Of those that a mesh axis runs over, the one named last changes fastest.
Arguments:
- momentum: float32 [8192, 28672], P('tp', 'fsdp'), may hold values from -6 to 6
- gradient: bfloat16 [8192, 28672], P('tp', 'fsdp'), may hold values from -6 to 6
- basis: float32 [28672, 512], P('fsdp', 'tp'), may hold values from -1 to 1
Outputs:
- new_momentum: float32 [8192, 28672], P('tp', 'fsdp')
- new_basis: float32 [28672, 512], P('fsdp', 'tp')
- left_factor: float32 [8192, 512], P(('tp', 'fsdp'))
The draws below stay inside these ranges and needn't reach their ends.
All inputs are finite; a program needn't handle non-finite values.
Results may differ from the reference program's by a relative error of at most 0.0003.
Values sent between devices are 32-bit elements; how exact they have to be, the bound alone decides.
A program may use at most 192 MiB of HBM per device.

```python
import math
import jax
import jax.numpy as jnp
from jax import lax

D = 8192
FF = 28672
RANK = 512


def draw_basis(key, part):
    first_key, second_key, third_key = jax.random.split(jax.random.fold_in(key, 7301), 3)
    half_rank = RANK // 2
    leading = jax.random.uniform(first_key, (FF, half_rank), jnp.float32, -1.0, 1.0)
    fresh_noise = jax.random.uniform(second_key, (FF, half_rank), jnp.float32, -1.0, 1.0)
    mixing = jnp.exp(jax.random.uniform(third_key, (1, half_rank), jnp.float32, math.log(0.004), math.log(0.008)))
    partner = (1.0 - mixing) * leading + mixing * fresh_noise
    return jnp.stack([leading, partner], axis=2).reshape(FF, RANK).astype(jnp.float32)


def shard_levels(stream_key, shape, shards, least, largest):
    factor_of, own = 1.0, jax.random.fold_in(stream_key, 6)
    for position, shards_of in shards:
        draws = jnp.exp(jax.random.uniform(jax.random.fold_in(own, position), (shards_of,), jnp.float32, least / len(shards), largest / len(shards)))
        factor_of = factor_of * jnp.repeat(draws, shape[position] // shards_of).reshape([-1 if axis == position else 1 for axis in range(len(shape))])
    return factor_of


def bell_draw(rng, dims, deviation, most, pieces=(), kind=jnp.bfloat16):
    array = jax.random.normal(rng, dims, jnp.float32) * deviation
    if len(pieces) > 0:
        array = shard_levels(rng, dims, pieces, -0.22, 0.18) * array
    return jnp.clip(array, min=-most, max=most).astype(kind)


def setup_inputs(seed: int = 0) -> dict:
    key_list = jax.random.split(jax.random.key(seed), 4)
    return {
        "momentum": bell_draw(key_list[0], (D, FF), 1.0, 6.0, ((0, 4), (1, 8)), jnp.float32),
        "gradient": bell_draw(key_list[1], (D, FF), 1.0, 6.0, ((0, 4), (1, 8))),
        "basis": draw_basis(jax.random.fold_in(key_list[3], 71), 0),
    }


keep_rate = 0.95
tiny = 1e-06
high = lax.Precision.HIGHEST

def orthonormal(left):
    for turn in range(2):
        gram = jnp.dot(left.T.astype(jnp.float32), left.astype(jnp.float32), precision=high, preferred_element_type=jnp.float32)
        lower = jnp.linalg.cholesky(gram)
        left = jax.scipy.linalg.solve_triangular(lower, left.T, lower=True).T
    return left

def reference(momentum, gradient, basis):
    blended = momentum + gradient.astype(jnp.float32)
    sketch = jnp.dot(blended.astype(jnp.float32), basis.astype(jnp.float32), precision=high, preferred_element_type=jnp.float32)
    left_factor = orthonormal(sketch)
    right = jnp.dot(blended.T.astype(jnp.float32), left_factor.astype(jnp.float32), precision=high, preferred_element_type=jnp.float32)
    new_momentum = blended - (1.0 - keep_rate) * jnp.dot(left_factor.astype(jnp.float32), right.T.astype(jnp.float32), precision=high, preferred_element_type=jnp.float32)
    scales = jnp.sqrt(lax.optimization_barrier(jnp.sum(right * right, axis=0)) + tiny)
    new_basis = right / scales[None, :]
    return (new_momentum, new_basis, left_factor)
```

```python
import functools

import jax
import jax.numpy as jnp
from jax import lax
from jax.experimental import pallas as pl
from jax.experimental.pallas import tpu as pltpu
from jax.sharding import PartitionSpec as P

keep_rate = 0.95
tiny = 1e-06
highest = lax.Precision.HIGHEST
MESH = pl.DeviceIdType.MESH
BLOCK = 128
PANEL = 8
CHUNK = 256


def product(a, b, dims, precision=highest):
    return lax.dot_general(a, b, ((dims[:1], dims[1:]), ((), ())), precision=precision, preferred_element_type=jnp.float32)


def eliminate_block(m_ref):
    lanes = lax.broadcasted_iota(jnp.int32, (PANEL, BLOCK), 1)
    subs = lax.broadcasted_iota(jnp.int32, (PANEL, BLOCK), 0)
    rows = lax.broadcasted_iota(jnp.int32, (BLOCK, BLOCK), 0)
    columns = lax.broadcasted_iota(jnp.int32, (BLOCK, BLOCK), 1)
    for start in range(0, BLOCK, PANEL):
        panel = m_ref[start:start + PANEL, :]
        heads = [jnp.broadcast_to(panel[:, start + j:start + j + 1], (PANEL, BLOCK)) for j in range(PANEL)]
        for j in range(PANEL):
            head = heads[j]
            pivot = jnp.broadcast_to(head[j:j + 1, :], (PANEL, BLOCK))
            root = lax.rsqrt(pivot)
            root = root * (1.5 - 0.5 * (pivot * root) * root)
            factor = jnp.where(subs > j, head * root, 0.0)
            row = jnp.broadcast_to(panel[j:j + 1, :], (PANEL, BLOCK)) * root
            row = jnp.where(lanes == start + j, root, row)
            kept = jnp.where((lanes == start + j) & (subs > j), 0.0, panel)
            panel = jnp.where(subs == j, row, kept - factor * row)
            for later in range(j + 1, PANEL):
                scaled = jnp.broadcast_to(heads[later][j:j + 1, :], (PANEL, BLOCK)) * root
                heads[later] = heads[later] - factor * scaled
        m_ref[start:start + PANEL, :] = jnp.where(lanes > start + subs, 0.0, panel)
        stop = start + PANEL
        if stop < BLOCK:
            right = jnp.where(lanes >= stop, panel, 0.0)
            own = jnp.where((lanes > start + subs) & (lanes < stop), 0.0, panel)
            update = product(right, own, (0, 0))
            below = m_ref[stop:, :]
            fresh = (columns[stop:] >= start) & (columns[stop:] < stop)
            m_ref[stop:, :] = jnp.where(fresh, 0.0, below) - update[stop:, :]


def orthonormal_kernel(sizes, own_ref, next_ref, inverse_ref, packed, gathered, land0, land1, land2, sum0, sum1, sum2, m_ref,
                       send0, recv0, send1, recv1, send2, recv2, send3, recv3, send4, recv4, send5, recv5):
    chips, count = sizes
    n = own_ref.shape[1]
    t, f = lax.axis_index("tp"), lax.axis_index("fsdp")
    y, c = t // 2, t % 2
    stages = [
        (2, c, lambda i: {"tp": 2 * y + i}),
        (chips, y, lambda i: {"tp": 2 * i + c}),
        (count, f, lambda i: {"fsdp": i}),
    ]
    barrier = pltpu.get_barrier_semaphore()
    for members, me, device in stages:
        for step in range(1, members):
            pl.semaphore_signal(barrier, inc=1, device_id=device(lax.rem(me + step, members)), device_id_type=MESH)

    blocks = n // BLOCK
    place = 0
    places = {}
    for i in range(blocks):
        strip = product(own_ref[:, i * BLOCK:(i + 1) * BLOCK], own_ref[:, i * BLOCK:], (0, 0))
        for j in range(i, blocks):
            packed[place:place + BLOCK, :] = strip[:, (j - i) * BLOCK:(j - i + 1) * BLOCK]
            places[i, j] = place
            place += BLOCK
    pl.semaphore_wait(barrier, sum(members - 1 for members, _, _ in stages))

    def rows(index, size):
        return pl.ds(pl.multiple_of(index * size, size), size)

    def exchange(stage, pick, put, send, recv):
        members, me, device = stage
        copies = []
        for step in range(1, members):
            target = lax.rem(me + step, members)
            copies.append(pltpu.make_async_remote_copy(
                src_ref=pick(target), dst_ref=put(step), send_sem=send.at[step],
                recv_sem=recv.at[step], device_id=device(target), device_id_type=MESH))
        for copy in copies:
            copy.start()
        return copies

    started = []
    source, base, size = packed, 0, place
    downs = ((land0, sum0, send0, recv0), (land1, sum1, send1, recv1), (land2, sum2, send2, recv2))
    for stage, (land, total_ref, send, recv) in zip(stages, downs):
        members, me, _ = stage
        size = size // members
        copies = exchange(stage, lambda i: source.at[rows(i, size)], lambda step: land.at[step], send, recv)
        started += copies
        total = source[rows(me, size), :]
        for step in range(1, members):
            copies[step - 1].wait_recv()
            total = total + land[step]
        total_ref[...] = total
        base = base + me * size
        source = total_ref
    mine = pl.ds(pl.multiple_of(base, size), size)
    ups = ((send3, recv3), (send4, recv4), (send5, recv5))
    source = sum2
    gathered[mine, :] = total
    for stage, (send, recv) in zip(stages[::-1], ups):
        members, me, _ = stage
        spot = gathered.at[pl.ds(pl.multiple_of(base, size), size)]
        copies = exchange(stage, lambda i: source, lambda step: spot, send, recv)
        started += copies
        for copy in copies:
            copy.wait_recv()
        base = base - me * size
        size = size * members
        source = gathered.at[pl.ds(pl.multiple_of(base, size), size)]
    for copy in started:
        copy.wait_send()
    for i in range(blocks):
        for j in range(i, blocks):
            inverse_ref[i * BLOCK:(i + 1) * BLOCK, j * BLOCK:(j + 1) * BLOCK] = gathered[places[i, j]:places[i, j] + BLOCK, :]
    inverse_kernel(inverse_ref, m_ref)
    next_ref[...] = product(own_ref[...], inverse_ref[...], (1, 1))


def inverse_kernel(x_ref, m_ref):
    n = x_ref.shape[0]
    for start in range(0, n, BLOCK):
        stop = start + BLOCK
        m_ref[...] = x_ref[start:stop, start:stop]
        eliminate_block(m_ref)
        diagonal = m_ref[...]
        x_ref[start:stop, start:stop] = diagonal
        if start > 0:
            x_ref[start:stop, :start] = product(diagonal, x_ref[start:stop, :start], (1, 0))
        if stop < n:
            right = product(diagonal, x_ref[start:stop, stop:], (1, 0))
            if start > 0:
                x_ref[stop:, :start] -= product(right, x_ref[start:stop, :start], (0, 0))
            x_ref[stop:, start:stop] = -product(right, diagonal, (0, 0))
            x_ref[stop:, stop:] -= product(right, right, (0, 0))
            x_ref[start:stop, stop:] = jnp.zeros((BLOCK, n - stop), jnp.float32)


def orthonormal_step(own, chips, count):
    rows, n = own.shape
    blocks = n // BLOCK
    packed = BLOCK * blocks * (blocks + 1) // 2
    dma = pltpu.SemaphoreType.DMA
    f32 = jnp.float32
    half, part = packed // 2, packed // 2 // chips
    return pl.pallas_call(
        functools.partial(orthonormal_kernel, (chips, count)),
        out_shape=[jax.ShapeDtypeStruct((rows, n), f32), jax.ShapeDtypeStruct((n, n), f32)],
        in_specs=[pl.BlockSpec(memory_space=pltpu.VMEM)],
        out_specs=[pl.BlockSpec(memory_space=pltpu.VMEM)] * 2,
        scratch_shapes=[
            pltpu.VMEM((packed, BLOCK), f32),
            pltpu.VMEM((packed, BLOCK), f32),
            pltpu.VMEM((2, half, BLOCK), f32),
            pltpu.VMEM((chips, part, BLOCK), f32),
            pltpu.VMEM((count, part // count, BLOCK), f32),
            pltpu.VMEM((half, BLOCK), f32),
            pltpu.VMEM((part, BLOCK), f32),
            pltpu.VMEM((part // count, BLOCK), f32),
            pltpu.VMEM((BLOCK, BLOCK), f32),
        ] + [dma((members,)) for members in (2, 2, chips, chips, count, count, count, count, chips, chips, 2, 2)],
        compiler_params=pltpu.CompilerParams(collective_id=2, has_side_effects=True),
        cost_estimate=pl.CostEstimate(flops=2 * n * n * n * 20, bytes_accessed=8 * n * n, transcendentals=n),
        name="orthonormal_step",
    )(own)


def inverse_factor(gram):
    n = gram.shape[0]

    def kernel(g_ref, x_ref, m_ref):
        x_ref[...] = g_ref[...]
        inverse_kernel(x_ref, m_ref)

    return pl.pallas_call(
        kernel,
        out_shape=jax.ShapeDtypeStruct((n, n), jnp.float32),
        in_specs=[pl.BlockSpec(memory_space=pltpu.VMEM)],
        out_specs=pl.BlockSpec(memory_space=pltpu.VMEM),
        scratch_shapes=[pltpu.VMEM((BLOCK, BLOCK), jnp.float32)],
        cost_estimate=pl.CostEstimate(flops=2 * n * n * n * 20, bytes_accessed=8 * n * n, transcendentals=n),
        name="inverse_factor",
    )(gram)


def pieces_of(value):
    high = value.astype(jnp.bfloat16)
    rest = value - high.astype(jnp.float32)
    middle = rest.astype(jnp.bfloat16)
    low = (rest - middle.astype(jnp.float32)).astype(jnp.bfloat16)
    return high, middle, low


def sketch_kernel(m_hbm, g_hbm, b_hbm, out_ref, m_buf, g_buf, land, split, part, land_x, summed, land_z,
                  m_sem, g_sem, own_sem, core_send, core_recv, y_send, y_recv, relay_send, relay_recv,
                  x_send, x_recv, z_send, z_recv):
    t, f = lax.axis_index("tp"), lax.axis_index("fsdp")
    y, c = t // 2, t % 2
    z, x = f // 2, f % 2
    width = b_hbm.shape[1]
    depth = m_hbm.shape[1]
    half = depth // 2
    block = m_hbm.shape[0] // 4
    own = block // 2
    core_peer = {"tp": 2 * y + 1 - c}
    y_peer = {"tp": 2 * (1 - y) + c}
    x_peer = {"fsdp": 2 * z + 1 - x}

    def order(j):
        return 2 * ((z // 2 + (3 - j) // 2) % 2) + (z % 2 + (3 - j) % 2) % 2

    barrier = pltpu.get_barrier_semaphore()
    for peer in [core_peer, y_peer, x_peer] + [{"fsdp": 2 * order(j) + x} for j in range(3)]:
        pl.semaphore_signal(barrier, inc=1, device_id=peer, device_id_type=MESH)

    def fetch(s):
        j = s % 4 * (s // 8) + (s // 2) * (1 - s // 8)
        k = (s % 2) * (1 - s // 8) + (s // 12)
        slot = s % 2
        rows = pl.ds(pl.multiple_of(order(j) * block, block), block)
        columns = pl.ds(pl.multiple_of(k * half, half), half)
        return (pltpu.make_async_copy(m_hbm.at[rows, columns], m_buf.at[slot], m_sem.at[slot]),
                pltpu.make_async_copy(g_hbm.at[rows, columns], g_buf.at[slot], g_sem.at[slot]))

    own_copy = pltpu.make_async_copy(b_hbm, land.at[0], own_sem)
    own_copy.start()
    for copy in fetch(0):
        copy.start()
    pl.semaphore_wait(barrier, 6)

    quarter = depth // 4

    def remote(source, target, send, recv, peer):
        return pltpu.make_async_remote_copy(src_ref=source, dst_ref=target, send_sem=send, recv_sem=recv,
                                            device_id=peer, device_id_type=MESH)

    to_core = [remote(b_hbm.at[pl.ds(k * half, half)], land.at[1, pl.ds(k * half, half)],
                      core_send.at[k], core_recv.at[k], core_peer) for k in range(2)]
    to_y = [remote(b_hbm.at[pl.ds(q * quarter, quarter)], land.at[2, pl.ds(q * quarter, quarter)],
                   y_send.at[q], y_recv.at[q], y_peer) for q in range(4)]
    relay = [remote(land.at[2, pl.ds(q * quarter, quarter)], land.at[3, pl.ds(q * quarter, quarter)],
                    relay_send.at[q], relay_recv.at[q], core_peer) for q in range(4)]
    for copy in to_core + to_y:
        copy.start()

    def cut(slot, column, k):
        columns = pl.ds(pl.multiple_of(column * width, width), width)

        def body(i, carry):
            rows = pl.ds(pl.multiple_of(k * half + i * CHUNK, CHUNK), CHUNK)
            high, middle, low = pieces_of(land[slot, rows, :])
            for place, piece in enumerate((high, middle, low, high, middle, high)):
                split[k, i, place * CHUNK:(place + 1) * CHUNK, columns] = piece
            return carry

        lax.fori_loop(0, half // CHUNK, body, 0)

    part[...] = jnp.zeros_like(part)
    own_copy.wait()
    cut(0, c, 0)
    to_core[0].wait_recv()
    cut(1, 1 - c, 0)

    across = [[remote(part.at[n, j, pl.ds(pl.multiple_of((1 - x) * own, own), own)], land_x.at[n, j],
                      x_send.at[n, j], x_recv.at[n, j], x_peer) for j in range(4)] for n in range(2)]
    along = [[remote(summed.at[n, j], land_z.at[n, j], z_send.at[n, j], z_recv.at[n, j],
                     {"fsdp": 2 * order(j) + x}) for j in range(3)] for n in range(2)]

    def add_x(n, j):
        across[n][j].wait_recv()

        def body(i, carry):
            rows = pl.ds(pl.multiple_of(i * 64, 64), 64)
            mine = pl.ds(pl.multiple_of(x * own + i * 64, 64), 64)
            summed[n, j, rows, :] = part[n, j, mine, :] + land_x[n, j, rows, :]
            return carry

        lax.fori_loop(0, own // 64, body, 0)
        if j < 3:
            along[n][j].start()

    before = {}
    after = {}

    def at(table, s, action):
        table.setdefault(s, []).append(action)

    def second_half():
        cut(0, c, 1)
        to_core[1].wait_recv()
        cut(1, 1 - c, 1)

    def pass_on(q):
        to_y[q].wait_recv()
        relay[q].start()

    def other_chip(k):
        cut(2, c, k)
        relay[2 * k].wait_recv()
        relay[2 * k + 1].wait_recv()
        cut(3, 1 - c, k)

    at(before, 1, second_half)
    at(before, 4, lambda: pass_on(0))
    at(before, 7, lambda: pass_on(1))
    at(before, 8, lambda: other_chip(0))
    at(before, 10, lambda: pass_on(2))
    at(before, 12, lambda: pass_on(3))
    at(before, 12, lambda: other_chip(1))
    for j in range(4):
        at(after, 2 * j + 1, lambda j=j: across[0][j].start())
        at(after, 2 * j + 3, lambda j=j: add_x(0, j))
        at(after, 12 + j, lambda j=j: across[1][j].start())
    at(after, 14, lambda: add_x(1, 0))
    at(after, 15, lambda: add_x(1, 1))

    def step(s, carry):
        for copy in fetch(s):
            copy.wait()

        @pl.when(s < 15)
        def _():
            for copy in fetch(s + 1):
                copy.start()

        for when, actions in before.items():
            @pl.when(s == when)
            def _(actions=actions):
                for action in actions:
                    action()

        slot = s % 2
        j = s % 4 * (s // 8) + (s // 2) * (1 - s // 8)
        k = (s % 2) * (1 - s // 8) + (s // 12)
        n = s // 8

        def body(i, inner):
            columns = pl.ds(pl.multiple_of(i * CHUNK, CHUNK), CHUNK)
            value = m_buf[slot, :, columns] + g_buf[slot, :, columns].astype(jnp.float32)
            high, middle, low = pieces_of(value)
            left = jnp.concatenate([high, high, high, middle, middle, low], axis=1)
            part[n, j] += jnp.dot(left, split[k, i], preferred_element_type=jnp.float32)
            return inner

        lax.fori_loop(0, half // CHUNK, body, 0)
        for when, actions in after.items():
            @pl.when(s == when)
            def _(actions=actions):
                for action in actions:
                    action()
        return carry

    lax.fori_loop(0, 16, step, 0)
    add_x(1, 2)
    add_x(1, 3)
    for n in range(2):
        for j in range(3):
            along[n][j].wait_recv()
        columns = pl.ds(pl.multiple_of((y * (1 - n) + (1 - y) * n) * 2 * width, 2 * width), 2 * width)
        out_ref[:, columns] = summed[n, 3] + land_z[n, 0] + land_z[n, 1] + land_z[n, 2]
    for copy in to_core + to_y + relay + across[0] + across[1] + along[0] + along[1]:
        copy.wait_send()


def sketch_rows(momentum, gradient, basis):
    rows, depth = momentum.shape
    width = basis.shape[1]
    block, half = rows // 4, depth // 2
    own = block // 2
    dma = pltpu.SemaphoreType.DMA
    f32 = jnp.float32
    return pl.pallas_call(
        sketch_kernel,
        out_shape=jax.ShapeDtypeStruct((own, 4 * width), f32),
        in_specs=[pl.BlockSpec(memory_space=pl.ANY)] * 3,
        out_specs=pl.BlockSpec(memory_space=pltpu.VMEM),
        scratch_shapes=[
            pltpu.VMEM((2, block, half), f32),
            pltpu.VMEM((2, block, half), jnp.bfloat16),
            pltpu.VMEM((4, depth, width), f32),
            pltpu.VMEM((2, half // CHUNK, 6 * CHUNK, 2 * width), jnp.bfloat16),
            pltpu.VMEM((2, 4, block, 2 * width), f32),
            pltpu.VMEM((2, 4, own, 2 * width), f32),
            pltpu.VMEM((2, 4, own, 2 * width), f32),
            pltpu.VMEM((2, 3, own, 2 * width), f32),
            dma((2,)), dma((2,)), dma, dma((2,)), dma((2,)), dma((4,)), dma((4,)), dma((4,)), dma((4,)),
            dma((2, 4)), dma((2, 4)), dma((2, 3)), dma((2, 3)),
        ],
        compiler_params=pltpu.CompilerParams(collective_id=1, has_side_effects=True, vmem_limit_bytes=60 * 1024 * 1024),
        cost_estimate=pl.CostEstimate(flops=12 * rows * depth * 4 * width, bytes_accessed=12 * rows * depth, transcendentals=0),
        name="sketch_rows",
    )(momentum, gradient, basis)


def sketch_own(momentum, gradient, basis, fitting):
    if fitting:
        return sketch_rows(momentum, gradient, basis)
    tile = momentum + gradient.astype(jnp.float32)
    partial_sketch = product(tile, lax.all_gather(basis, "tp", axis=1, tiled=True), (1, 0))
    return lax.psum_scatter(partial_sketch, "fsdp", scatter_dimension=0, tiled=True)


def orthonormal(own, fitting):
    if fitting:
        return orthonormal_step(own, lax.axis_size("tp") // 2, lax.axis_size("fsdp"))
    inverse = inverse_factor(lax.psum(product(own, own, (0, 0)), ("fsdp", "tp")))
    return product(own, inverse, (1, 1)), inverse


def on_device(momentum, gradient, basis):
    fitting = lax.axis_size("tp") == 4 and lax.axis_size("fsdp") == 8
    own = sketch_own(momentum, gradient, basis, fitting)
    sketch = lax.all_gather(own, "fsdp", axis=0, tiled=True)
    own_first, inverse = orthonormal(own, fitting)
    own_left, second = orthonormal(own_first, fitting)
    left = product(sketch, product(second, inverse, (1, 0)), (1, 1))
    tile = momentum + gradient.astype(jnp.float32)
    partial_right = product(tile, left, (0, 0), lax.Precision.HIGH)
    mine = lax.psum_scatter(partial_right, "tp", scatter_dimension=1, tiled=True)
    squares = lax.psum(jnp.sum(mine * mine, axis=0), "fsdp")
    new_basis = mine / jnp.sqrt(squares + tiny)[None, :]
    full_right = lax.all_gather(mine, "tp", axis=1, tiled=True)
    new_momentum = tile - product(left, (1.0 - keep_rate) * full_right, (1, 1), lax.Precision.DEFAULT)
    return (new_momentum, new_basis, own_left)


def solution(mesh):
    placed = (P("tp", "fsdp"), P("tp", "fsdp"), P("fsdp", "tp"))
    return jax.shard_map(
        on_device,
        mesh=mesh,
        in_specs=placed,
        out_specs=(P("tp", "fsdp"), P("fsdp", "tp"), P(("tp", "fsdp"), None)),
        check_vma=False,
    )
```

```python
import functools

import jax
import jax.numpy as jnp
from jax import lax
from jax.experimental import pallas as pl
from jax.experimental.pallas import tpu as pltpu
from jax.sharding import PartitionSpec as P

keep_rate = 0.95
tiny = 1e-06
highest = lax.Precision.HIGHEST
MESH = pl.DeviceIdType.MESH
BLOCK = 128
PANEL = 8
CHUNK = 256


def product(a, b, dims, precision=highest):
    return lax.dot_general(a, b, ((dims[:1], dims[1:]), ((), ())), precision=precision, preferred_element_type=jnp.float32)


def eliminate_block(m_ref):
    lanes = lax.broadcasted_iota(jnp.int32, (PANEL, BLOCK), 1)
    subs = lax.broadcasted_iota(jnp.int32, (PANEL, BLOCK), 0)
    rows = lax.broadcasted_iota(jnp.int32, (BLOCK, BLOCK), 0)
    columns = lax.broadcasted_iota(jnp.int32, (BLOCK, BLOCK), 1)
    for start in range(0, BLOCK, PANEL):
        panel = m_ref[start:start + PANEL, :]
        heads = [jnp.broadcast_to(panel[:, start + j:start + j + 1], (PANEL, BLOCK)) for j in range(PANEL)]
        for j in range(PANEL):
            head = heads[j]
            pivot = jnp.broadcast_to(head[j:j + 1, :], (PANEL, BLOCK))
            root = lax.rsqrt(pivot)
            root = root * (1.5 - 0.5 * (pivot * root) * root)
            factor = jnp.where(subs > j, head * root, 0.0)
            row = jnp.broadcast_to(panel[j:j + 1, :], (PANEL, BLOCK)) * root
            row = jnp.where(lanes == start + j, root, row)
            kept = jnp.where((lanes == start + j) & (subs > j), 0.0, panel)
            panel = jnp.where(subs == j, row, kept - factor * row)
            for later in range(j + 1, PANEL):
                scaled = jnp.broadcast_to(heads[later][j:j + 1, :], (PANEL, BLOCK)) * root
                heads[later] = heads[later] - factor * scaled
        m_ref[start:start + PANEL, :] = jnp.where(lanes > start + subs, 0.0, panel)
        stop = start + PANEL
        if stop < BLOCK:
            right = jnp.where(lanes >= stop, panel, 0.0)
            own = jnp.where((lanes > start + subs) & (lanes < stop), 0.0, panel)
            update = product(right, own, (0, 0))
            below = m_ref[stop:, :]
            fresh = (columns[stop:] >= start) & (columns[stop:] < stop)
            m_ref[stop:, :] = jnp.where(fresh, 0.0, below) - update[stop:, :]


def orthonormal_kernel(sizes, own_ref, next_ref, inverse_ref, packed, gathered, land0, land1, land2, sum0, sum1, sum2, m_ref,
                       send0, recv0, send1, recv1, send2, recv2, send3, recv3, send4, recv4, send5, recv5):
    chips, count = sizes
    n = own_ref.shape[1]
    t, f = lax.axis_index("tp"), lax.axis_index("fsdp")
    y, c = t // 2, t % 2
    stages = [
        (2, c, lambda i: {"tp": 2 * y + i}),
        (chips, y, lambda i: {"tp": 2 * i + c}),
        (count, f, lambda i: {"fsdp": i}),
    ]
    barrier = pltpu.get_barrier_semaphore()
    for members, me, device in stages:
        for step in range(1, members):
            pl.semaphore_signal(barrier, inc=1, device_id=device(lax.rem(me + step, members)), device_id_type=MESH)

    blocks = n // BLOCK
    place = 0
    places = {}
    for i in range(blocks):
        strip = product(own_ref[:, i * BLOCK:(i + 1) * BLOCK], own_ref[:, i * BLOCK:], (0, 0))
        for j in range(i, blocks):
            packed[place:place + BLOCK, :] = strip[:, (j - i) * BLOCK:(j - i + 1) * BLOCK]
            places[i, j] = place
            place += BLOCK
    pl.semaphore_wait(barrier, sum(members - 1 for members, _, _ in stages))

    def rows(index, size):
        return pl.ds(pl.multiple_of(index * size, size), size)

    def exchange(stage, pick, put, send, recv):
        members, me, device = stage
        copies = []
        for step in range(1, members):
            target = lax.rem(me + step, members)
            copies.append(pltpu.make_async_remote_copy(
                src_ref=pick(target), dst_ref=put(step), send_sem=send.at[step],
                recv_sem=recv.at[step], device_id=device(target), device_id_type=MESH))
        for copy in copies:
            copy.start()
        return copies

    started = []
    source, base, size = packed, 0, place
    downs = ((land0, sum0, send0, recv0), (land1, sum1, send1, recv1), (land2, sum2, send2, recv2))
    for stage, (land, total_ref, send, recv) in zip(stages, downs):
        members, me, _ = stage
        size = size // members
        copies = exchange(stage, lambda i: source.at[rows(i, size)], lambda step: land.at[step], send, recv)
        started += copies
        total = source[rows(me, size), :]
        for step in range(1, members):
            copies[step - 1].wait_recv()
            total = total + land[step]
        total_ref[...] = total
        base = base + me * size
        source = total_ref
    mine = pl.ds(pl.multiple_of(base, size), size)
    ups = ((send3, recv3), (send4, recv4), (send5, recv5))
    source = sum2
    gathered[mine, :] = total
    for stage, (send, recv) in zip(stages[::-1], ups):
        members, me, _ = stage
        spot = gathered.at[pl.ds(pl.multiple_of(base, size), size)]
        copies = exchange(stage, lambda i: source, lambda step: spot, send, recv)
        started += copies
        for copy in copies:
            copy.wait_recv()
        base = base - me * size
        size = size * members
        source = gathered.at[pl.ds(pl.multiple_of(base, size), size)]
    for copy in started:
        copy.wait_send()
    for i in range(blocks):
        for j in range(i, blocks):
            inverse_ref[i * BLOCK:(i + 1) * BLOCK, j * BLOCK:(j + 1) * BLOCK] = gathered[places[i, j]:places[i, j] + BLOCK, :]
    inverse_kernel(inverse_ref, m_ref)
    next_ref[...] = product(own_ref[...], inverse_ref[...], (1, 1))


def inverse_kernel(x_ref, m_ref):
    n = x_ref.shape[0]
    for start in range(0, n, BLOCK):
        stop = start + BLOCK
        m_ref[...] = x_ref[start:stop, start:stop]
        eliminate_block(m_ref)
        diagonal = m_ref[...]
        x_ref[start:stop, start:stop] = diagonal
        if start > 0:
            x_ref[start:stop, :start] = product(diagonal, x_ref[start:stop, :start], (1, 0))
        if stop < n:
            right = product(diagonal, x_ref[start:stop, stop:], (1, 0))
            if start > 0:
                x_ref[stop:, :start] -= product(right, x_ref[start:stop, :start], (0, 0))
            x_ref[stop:, start:stop] = -product(right, diagonal, (0, 0))
            x_ref[stop:, stop:] -= product(right, right, (0, 0))
            x_ref[start:stop, stop:] = jnp.zeros((BLOCK, n - stop), jnp.float32)


def orthonormal_step(own, chips, count):
    rows, n = own.shape
    blocks = n // BLOCK
    packed = BLOCK * blocks * (blocks + 1) // 2
    dma = pltpu.SemaphoreType.DMA
    f32 = jnp.float32
    half, part = packed // 2, packed // 2 // chips
    return pl.pallas_call(
        functools.partial(orthonormal_kernel, (chips, count)),
        out_shape=[jax.ShapeDtypeStruct((rows, n), f32), jax.ShapeDtypeStruct((n, n), f32)],
        in_specs=[pl.BlockSpec(memory_space=pltpu.VMEM)],
        out_specs=[pl.BlockSpec(memory_space=pltpu.VMEM)] * 2,
        scratch_shapes=[
            pltpu.VMEM((packed, BLOCK), f32),
            pltpu.VMEM((packed, BLOCK), f32),
            pltpu.VMEM((2, half, BLOCK), f32),
            pltpu.VMEM((chips, part, BLOCK), f32),
            pltpu.VMEM((count, part // count, BLOCK), f32),
            pltpu.VMEM((half, BLOCK), f32),
            pltpu.VMEM((part, BLOCK), f32),
            pltpu.VMEM((part // count, BLOCK), f32),
            pltpu.VMEM((BLOCK, BLOCK), f32),
        ] + [dma((members,)) for members in (2, 2, chips, chips, count, count, count, count, chips, chips, 2, 2)],
        compiler_params=pltpu.CompilerParams(collective_id=2, has_side_effects=True),
        cost_estimate=pl.CostEstimate(flops=2 * n * n * n * 20, bytes_accessed=8 * n * n, transcendentals=n),
        name="orthonormal_step",
    )(own)


def inverse_factor(gram):
    n = gram.shape[0]

    def kernel(g_ref, x_ref, m_ref):
        x_ref[...] = g_ref[...]
        inverse_kernel(x_ref, m_ref)

    return pl.pallas_call(
        kernel,
        out_shape=jax.ShapeDtypeStruct((n, n), jnp.float32),
        in_specs=[pl.BlockSpec(memory_space=pltpu.VMEM)],
        out_specs=pl.BlockSpec(memory_space=pltpu.VMEM),
        scratch_shapes=[pltpu.VMEM((BLOCK, BLOCK), jnp.float32)],
        cost_estimate=pl.CostEstimate(flops=2 * n * n * n * 20, bytes_accessed=8 * n * n, transcendentals=n),
        name="inverse_factor",
    )(gram)


def pieces_of(value):
    high = value.astype(jnp.bfloat16)
    rest = value - high.astype(jnp.float32)
    middle = rest.astype(jnp.bfloat16)
    low = (rest - middle.astype(jnp.float32)).astype(jnp.bfloat16)
    return high, middle, low


def sketch_kernel(m_hbm, g_hbm, b_hbm, out_ref, m_buf, g_buf, land, split, part, land_x, summed, land_z,
                  m_sem, g_sem, own_sem, core_send, core_recv, y_send, y_recv, relay_send, relay_recv,
                  x_send, x_recv, z_send, z_recv):
    t, f = lax.axis_index("tp"), lax.axis_index("fsdp")
    y, c = t // 2, t % 2
    z, x = f // 2, f % 2
    width = b_hbm.shape[1]
    depth = m_hbm.shape[1]
    half = depth // 2
    block = m_hbm.shape[0] // 4
    own = block // 2
    core_peer = {"tp": 2 * y + 1 - c}
    y_peer = {"tp": 2 * (1 - y) + c}
    x_peer = {"fsdp": 2 * z + 1 - x}

    def order(j):
        return 2 * ((z // 2 + (3 - j) // 2) % 2) + (z % 2 + (3 - j) % 2) % 2

    barrier = pltpu.get_barrier_semaphore()
    for peer in [core_peer, y_peer, x_peer] + [{"fsdp": 2 * order(j) + x} for j in range(3)]:
        pl.semaphore_signal(barrier, inc=1, device_id=peer, device_id_type=MESH)

    def fetch(s):
        j = s % 4 * (s // 8) + (s // 2) * (1 - s // 8)
        k = (s % 2) * (1 - s // 8) + (s // 12)
        slot = s % 2
        rows = pl.ds(pl.multiple_of(order(j) * block, block), block)
        columns = pl.ds(pl.multiple_of(k * half, half), half)
        return (pltpu.make_async_copy(m_hbm.at[rows, columns], m_buf.at[slot], m_sem.at[slot]),
                pltpu.make_async_copy(g_hbm.at[rows, columns], g_buf.at[slot], g_sem.at[slot]))

    own_copy = pltpu.make_async_copy(b_hbm, land.at[0], own_sem)
    own_copy.start()
    for copy in fetch(0):
        copy.start()
    pl.semaphore_wait(barrier, 6)

    quarter = depth // 4

    def remote(source, target, send, recv, peer):
        return pltpu.make_async_remote_copy(src_ref=source, dst_ref=target, send_sem=send, recv_sem=recv,
                                            device_id=peer, device_id_type=MESH)

    to_core = [remote(b_hbm.at[pl.ds(k * half, half)], land.at[1, pl.ds(k * half, half)],
                      core_send.at[k], core_recv.at[k], core_peer) for k in range(2)]
    to_y = [remote(b_hbm.at[pl.ds(q * quarter, quarter)], land.at[2, pl.ds(q * quarter, quarter)],
                   y_send.at[q], y_recv.at[q], y_peer) for q in range(4)]
    relay = [remote(land.at[2, pl.ds(q * quarter, quarter)], land.at[3, pl.ds(q * quarter, quarter)],
                    relay_send.at[q], relay_recv.at[q], core_peer) for q in range(4)]
    for copy in to_core + to_y:
        copy.start()

    def cut(slot, column, k):
        columns = pl.ds(pl.multiple_of(column * width, width), width)

        def body(i, carry):
            rows = pl.ds(pl.multiple_of(k * half + i * CHUNK, CHUNK), CHUNK)
            high, middle, low = pieces_of(land[slot, rows, :])
            for place, piece in enumerate((high, middle, low, high, middle, high)):
                split[k, i, place * CHUNK:(place + 1) * CHUNK, columns] = piece
            return carry

        lax.fori_loop(0, half // CHUNK, body, 0)

    part[...] = jnp.zeros_like(part)
    own_copy.wait()
    cut(0, c, 0)
    to_core[0].wait_recv()
    cut(1, 1 - c, 0)

    across = [[remote(part.at[n, j, pl.ds(pl.multiple_of((1 - x) * own, own), own)], land_x.at[n, j],
                      x_send.at[n, j], x_recv.at[n, j], x_peer) for j in range(4)] for n in range(2)]
    along = [[remote(summed.at[n, j], land_z.at[n, j], z_send.at[n, j], z_recv.at[n, j],
                     {"fsdp": 2 * order(j) + x}) for j in range(3)] for n in range(2)]

    def add_x(n, j):
        across[n][j].wait_recv()

        def body(i, carry):
            rows = pl.ds(pl.multiple_of(i * 64, 64), 64)
            mine = pl.ds(pl.multiple_of(x * own + i * 64, 64), 64)
            summed[n, j, rows, :] = part[n, j, mine, :] + land_x[n, j, rows, :]
            return carry

        lax.fori_loop(0, own // 64, body, 0)
        if j < 3:
            along[n][j].start()

    before = {}
    after = {}

    def at(table, s, action):
        table.setdefault(s, []).append(action)

    def second_half():
        cut(0, c, 1)
        to_core[1].wait_recv()
        cut(1, 1 - c, 1)

    def pass_on(q):
        to_y[q].wait_recv()
        relay[q].start()

    def other_chip(k):
        cut(2, c, k)
        relay[2 * k].wait_recv()
        relay[2 * k + 1].wait_recv()
        cut(3, 1 - c, k)

    at(before, 1, second_half)
    at(before, 4, lambda: pass_on(0))
    at(before, 7, lambda: pass_on(1))
    at(before, 8, lambda: other_chip(0))
    at(before, 10, lambda: pass_on(2))
    at(before, 12, lambda: pass_on(3))
    at(before, 12, lambda: other_chip(1))
    for j in range(4):
        at(after, 2 * j + 1, lambda j=j: across[0][j].start())
        at(after, 2 * j + 3, lambda j=j: add_x(0, j))
        at(after, 12 + j, lambda j=j: across[1][j].start())
    at(after, 14, lambda: add_x(1, 0))
    at(after, 15, lambda: add_x(1, 1))

    def step(s, carry):
        for copy in fetch(s):
            copy.wait()

        @pl.when(s < 15)
        def _():
            for copy in fetch(s + 1):
                copy.start()

        for when, actions in before.items():
            @pl.when(s == when)
            def _(actions=actions):
                for action in actions:
                    action()

        slot = s % 2
        j = s % 4 * (s // 8) + (s // 2) * (1 - s // 8)
        k = (s % 2) * (1 - s // 8) + (s // 12)
        n = s // 8

        def body(i, inner):
            columns = pl.ds(pl.multiple_of(i * CHUNK, CHUNK), CHUNK)
            value = m_buf[slot, :, columns] + g_buf[slot, :, columns].astype(jnp.float32)
            high, middle, low = pieces_of(value)
            left = jnp.concatenate([high, high, high, middle, middle, low], axis=1)
            part[n, j] += jnp.dot(left, split[k, i], preferred_element_type=jnp.float32)
            return inner

        lax.fori_loop(0, half // CHUNK, body, 0)
        for when, actions in after.items():
            @pl.when(s == when)
            def _(actions=actions):
                for action in actions:
                    action()
        return carry

    lax.fori_loop(0, 16, step, 0)
    add_x(1, 2)
    add_x(1, 3)
    for n in range(2):
        for j in range(3):
            along[n][j].wait_recv()
        columns = pl.ds(pl.multiple_of((y * (1 - n) + (1 - y) * n) * 2 * width, 2 * width), 2 * width)
        out_ref[:, columns] = summed[n, 3] + land_z[n, 0] + land_z[n, 1] + land_z[n, 2]
    for copy in to_core + to_y + relay + across[0] + across[1] + along[0] + along[1]:
        copy.wait_send()


def sketch_rows(momentum, gradient, basis):
    rows, depth = momentum.shape
    width = basis.shape[1]
    block, half = rows // 4, depth // 2
    own = block // 2
    dma = pltpu.SemaphoreType.DMA
    f32 = jnp.float32
    return pl.pallas_call(
        sketch_kernel,
        out_shape=jax.ShapeDtypeStruct((own, 4 * width), f32),
        in_specs=[pl.BlockSpec(memory_space=pl.ANY)] * 3,
        out_specs=pl.BlockSpec(memory_space=pltpu.VMEM),
        scratch_shapes=[
            pltpu.VMEM((2, block, half), f32),
            pltpu.VMEM((2, block, half), jnp.bfloat16),
            pltpu.VMEM((4, depth, width), f32),
            pltpu.VMEM((2, half // CHUNK, 6 * CHUNK, 2 * width), jnp.bfloat16),
            pltpu.VMEM((2, 4, block, 2 * width), f32),
            pltpu.VMEM((2, 4, own, 2 * width), f32),
            pltpu.VMEM((2, 4, own, 2 * width), f32),
            pltpu.VMEM((2, 3, own, 2 * width), f32),
            dma((2,)), dma((2,)), dma, dma((2,)), dma((2,)), dma((4,)), dma((4,)), dma((4,)), dma((4,)),
            dma((2, 4)), dma((2, 4)), dma((2, 3)), dma((2, 3)),
        ],
        compiler_params=pltpu.CompilerParams(collective_id=1, has_side_effects=True, vmem_limit_bytes=60 * 1024 * 1024),
        cost_estimate=pl.CostEstimate(flops=12 * rows * depth * 4 * width, bytes_accessed=12 * rows * depth, transcendentals=0),
        name="sketch_rows",
    )(momentum, gradient, basis)


def right_kernel(count, m_hbm, g_hbm, left_ref, right_ref, basis_ref, m_buf, g_buf, high_ref, low_ref, part, land_c, summed, land_y,
                 rows_ref, squares, land_s, m_sem, g_sem, core_send, core_recv, y_send, y_recv, keep_send, keep_recv,
                 over_send, over_recv, relay_send, relay_recv, s_send, s_recv):
    t, f = lax.axis_index("tp"), lax.axis_index("fsdp")
    y, c = t // 2, t % 2
    rank, depth = left_ref.shape
    width = rank // 4
    steps = part.shape[0]
    core_peer = {"tp": 2 * y + 1 - c}
    y_peer = {"tp": 2 * (1 - y) + c}
    other = 2 * (1 - y) + c

    barrier = pltpu.get_barrier_semaphore()
    for peer in [core_peer, y_peer] + [{"fsdp": lax.rem(f + step, count)} for step in range(1, count)]:
        pl.semaphore_signal(barrier, inc=1, device_id=peer, device_id_type=MESH)

    def fetch(s):
        columns = pl.ds(pl.multiple_of(s * CHUNK, CHUNK), CHUNK)
        return (pltpu.make_async_copy(m_hbm.at[:, columns], m_buf.at[s % 2], m_sem.at[s % 2]),
                pltpu.make_async_copy(g_hbm.at[:, columns], g_buf.at[s % 2], g_sem.at[s % 2]))

    for copy in fetch(0):
        copy.start()

    def remote(source, target, send, recv, peer):
        return pltpu.make_async_remote_copy(src_ref=source, dst_ref=target, send_sem=send, recv_sem=recv,
                                            device_id=peer, device_id_type=MESH)

    def band(index):
        return pl.ds(pl.multiple_of(index * width, width), width)

    def spot(index, s):
        return right_ref.at[band(index), pl.ds(pl.multiple_of(s * CHUNK, CHUNK), CHUNK)]

    def to_core(s, chip):
        return remote(part.at[s, band(2 * chip + 1 - c)], land_c.at[s, chip], core_send.at[s, chip], core_recv.at[s, chip], core_peer)

    def to_y(s):
        return remote(summed.at[s, 1 - y], land_y.at[s], y_send.at[s], y_recv.at[s], y_peer)

    def keep(s):
        return remote(spot(t, s), spot(t, s), keep_send.at[s], keep_recv.at[s], core_peer)

    def over(s):
        return remote(spot(t, s), spot(t, s), over_send.at[s], over_recv.at[s], y_peer)

    def relay(s):
        return remote(spot(other, s), spot(other, s), relay_send.at[s], relay_recv.at[s], core_peer)

    def split(i, carry):
        columns = pl.ds(pl.multiple_of(i * CHUNK, CHUNK), CHUNK)
        value = left_ref[:, columns]
        high = value.astype(jnp.bfloat16)
        high_ref[i] = high
        low_ref[i] = (value - high.astype(jnp.float32)).astype(jnp.bfloat16)
        return carry

    lax.fori_loop(0, depth // CHUNK, split, 0)
    squares[...] = jnp.zeros_like(squares)
    pl.semaphore_wait(barrier, 1 + count)

    def step(s, carry):
        @pl.when(s < steps)
        def _():
            for copy in fetch(s):
                copy.wait()

            @pl.when(s < steps - 1)
            def _():
                for copy in fetch(s + 1):
                    copy.start()

            part[s] = jnp.zeros((rank, CHUNK), jnp.float32)

            def body(i, inner):
                rows = pl.ds(pl.multiple_of(i * CHUNK, CHUNK), CHUNK)
                value = m_buf[s % 2, rows, :] + g_buf[s % 2, rows, :].astype(jnp.float32)
                high = value.astype(jnp.bfloat16)
                low = (value - high.astype(jnp.float32)).astype(jnp.bfloat16)
                left = jnp.concatenate([high_ref[i], high_ref[i], low_ref[i]], axis=1)
                part[s] += jnp.dot(left, jnp.concatenate([high, low, high], axis=0), preferred_element_type=jnp.float32)
                return inner

            lax.fori_loop(0, depth // CHUNK, body, 0)
            for chip in range(2):
                to_core(s, chip).start()

        @pl.when((s >= 1) & (s < steps + 1))
        def _():
            now = s - 1
            for chip in range(2):
                to_core(now, chip).wait_recv()
                summed[now, chip] = part[now, band(2 * chip + c), :] + land_c[now, chip]
            to_y(now).start()

        @pl.when((s >= 4) & (s < steps + 4))
        def _():
            now = s - 4
            to_y(now).wait_recv()
            mine = summed[now, y] + land_y[now]
            right_ref[band(t), pl.ds(pl.multiple_of(now * CHUNK, CHUNK), CHUNK)] = mine
            over(now).start()
            keep(now).start()
            turned = mine.T
            rows_ref[pl.ds(pl.multiple_of(now * CHUNK, CHUNK), CHUNK), :] = turned
            squares[...] += jnp.sum((turned * turned).reshape(CHUNK // 8, 8, width), axis=0)

        @pl.when(s >= 7)
        def _():
            now = s - 7
            over(now).wait_recv()
            relay(now).start()
        return carry

    lax.fori_loop(0, steps + 4, step, 0)
    spread = [remote(squares, land_s.at[step], s_send.at[step], s_recv.at[step], {"fsdp": lax.rem(f + step, count)})
              for step in range(1, count)]
    for copy in spread:
        copy.start()
    total = squares[...]
    for step in range(1, count):
        spread[step - 1].wait_recv()
        total = total + land_s[step]
    scale = jnp.sqrt(jnp.sum(total, axis=0, keepdims=True) + tiny)

    def divide(i, carry):
        rows = pl.ds(pl.multiple_of(i * CHUNK, CHUNK), CHUNK)
        basis_ref[rows, :] = rows_ref[rows, :] / scale
        return carry

    lax.fori_loop(0, steps, divide, 0)

    def last(s, carry):
        over(s).wait_recv()
        relay(s).start()
        return carry

    lax.fori_loop(steps - 3, steps, last, 0)

    def drain(s, carry):
        for chip in range(2):
            to_core(s, chip).wait_send()
        to_y(s).wait_send()
        over(s).wait_send()
        keep(s).wait()
        relay(s).wait()
        return carry

    lax.fori_loop(0, steps, drain, 0)
    for copy in spread:
        copy.wait_send()


def right_columns(momentum, gradient, left, count):
    rows, depth = momentum.shape
    rank = left.shape[0]
    width = rank // 4
    steps = depth // CHUNK
    dma = pltpu.SemaphoreType.DMA
    f32 = jnp.float32
    return pl.pallas_call(
        functools.partial(right_kernel, count),
        out_shape=[jax.ShapeDtypeStruct((rank, depth), f32), jax.ShapeDtypeStruct((depth, width), f32)],
        in_specs=[pl.BlockSpec(memory_space=pl.ANY)] * 2 + [pl.BlockSpec(memory_space=pltpu.VMEM)],
        out_specs=[pl.BlockSpec(memory_space=pltpu.VMEM)] * 2,
        scratch_shapes=[
            pltpu.VMEM((2, rows, CHUNK), f32),
            pltpu.VMEM((2, rows, CHUNK), jnp.bfloat16),
            pltpu.VMEM((rows // CHUNK, rank, CHUNK), jnp.bfloat16),
            pltpu.VMEM((rows // CHUNK, rank, CHUNK), jnp.bfloat16),
            pltpu.VMEM((steps, rank, CHUNK), f32),
            pltpu.VMEM((steps, 2, width, CHUNK), f32),
            pltpu.VMEM((steps, 2, width, CHUNK), f32),
            pltpu.VMEM((steps, width, CHUNK), f32),
            pltpu.VMEM((depth, width), f32),
            pltpu.VMEM((8, width), f32),
            pltpu.VMEM((count, 8, width), f32),
            dma((2,)), dma((2,)), dma((steps, 2)), dma((steps, 2)), dma((steps,)), dma((steps,)), dma((steps,)), dma((steps,)),
            dma((steps,)), dma((steps,)), dma((steps,)), dma((steps,)), dma((count,)), dma((count,)),
        ],
        compiler_params=pltpu.CompilerParams(collective_id=3, has_side_effects=True, vmem_limit_bytes=60 * 1024 * 1024),
        cost_estimate=pl.CostEstimate(flops=6 * rows * depth * rank, bytes_accessed=6 * rows * depth, transcendentals=0),
        name="right_columns",
    )(momentum, gradient, left)


def sketch_own(momentum, gradient, basis, fitting):
    if fitting:
        return sketch_rows(momentum, gradient, basis)
    tile = momentum + gradient.astype(jnp.float32)
    partial_sketch = product(tile, lax.all_gather(basis, "tp", axis=1, tiled=True), (1, 0))
    return lax.psum_scatter(partial_sketch, "fsdp", scatter_dimension=0, tiled=True)


def orthonormal(own, fitting):
    if fitting:
        return orthonormal_step(own, lax.axis_size("tp") // 2, lax.axis_size("fsdp"))
    inverse = inverse_factor(lax.psum(product(own, own, (0, 0)), ("fsdp", "tp")))
    return product(own, inverse, (1, 1)), inverse


def on_device(momentum, gradient, basis):
    fitting = lax.axis_size("tp") == 4 and lax.axis_size("fsdp") == 8
    own = sketch_own(momentum, gradient, basis, fitting)
    sketch = lax.all_gather(own, "fsdp", axis=0, tiled=True)
    own_first, inverse = orthonormal(own, fitting)
    own_left, second = orthonormal(own_first, fitting)
    back = product(second, inverse, (1, 0))
    tile = momentum + gradient.astype(jnp.float32)
    if fitting:
        left = product(back, sketch, (1, 1))
        right, new_basis = right_columns(momentum, gradient, left, lax.axis_size("fsdp"))
        change = product(left, (1.0 - keep_rate) * right, (0, 0), lax.Precision.DEFAULT)
        return (tile - change, new_basis, own_left)
    left = product(sketch, back, (1, 1))
    partial_right = product(tile, left, (0, 0), lax.Precision.HIGH)
    mine = lax.psum_scatter(partial_right, "tp", scatter_dimension=1, tiled=True)
    squares = lax.psum(jnp.sum(mine * mine, axis=0), "fsdp")
    new_basis = mine / jnp.sqrt(squares + tiny)[None, :]
    full_right = lax.all_gather(mine, "tp", axis=1, tiled=True)
    new_momentum = tile - product(left, (1.0 - keep_rate) * full_right, (1, 1), lax.Precision.DEFAULT)
    return (new_momentum, new_basis, own_left)


def solution(mesh):
    placed = (P("tp", "fsdp"), P("tp", "fsdp"), P("fsdp", "tp"))
    return jax.shard_map(
        on_device,
        mesh=mesh,
        in_specs=placed,
        out_specs=(P("tp", "fsdp"), P("fsdp", "tp"), P(("tp", "fsdp"), None)),
        check_vma=False,
    )
```

```python
import functools

import jax
import jax.numpy as jnp
from jax import lax
from jax.experimental import pallas as pl
from jax.experimental.pallas import tpu as pltpu
from jax.sharding import PartitionSpec as P

keep_rate = 0.95
tiny = 1e-06
highest = lax.Precision.HIGHEST
MESH = pl.DeviceIdType.MESH
BLOCK = 128
PANEL = 8
CHUNK = 256


def product(a, b, dims, precision=highest):
    return lax.dot_general(a, b, ((dims[:1], dims[1:]), ((), ())), precision=precision, preferred_element_type=jnp.float32)


def eliminate_block(m_ref):
    lanes = lax.broadcasted_iota(jnp.int32, (PANEL, BLOCK), 1)
    subs = lax.broadcasted_iota(jnp.int32, (PANEL, BLOCK), 0)
    rows = lax.broadcasted_iota(jnp.int32, (BLOCK, BLOCK), 0)
    columns = lax.broadcasted_iota(jnp.int32, (BLOCK, BLOCK), 1)
    for start in range(0, BLOCK, PANEL):
        panel = m_ref[start:start + PANEL, :]
        heads = [jnp.broadcast_to(panel[:, start + j:start + j + 1], (PANEL, BLOCK)) for j in range(PANEL)]
        for j in range(PANEL):
            head = heads[j]
            pivot = jnp.broadcast_to(head[j:j + 1, :], (PANEL, BLOCK))
            root = lax.rsqrt(pivot)
            root = root * (1.5 - 0.5 * (pivot * root) * root)
            factor = jnp.where(subs > j, head * root, 0.0)
            row = jnp.broadcast_to(panel[j:j + 1, :], (PANEL, BLOCK)) * root
            row = jnp.where(lanes == start + j, root, row)
            kept = jnp.where((lanes == start + j) & (subs > j), 0.0, panel)
            panel = jnp.where(subs == j, row, kept - factor * row)
            for later in range(j + 1, PANEL):
                scaled = jnp.broadcast_to(heads[later][j:j + 1, :], (PANEL, BLOCK)) * root
                heads[later] = heads[later] - factor * scaled
        m_ref[start:start + PANEL, :] = jnp.where(lanes > start + subs, 0.0, panel)
        stop = start + PANEL
        if stop < BLOCK:
            right = jnp.where(lanes >= stop, panel, 0.0)
            own = jnp.where((lanes > start + subs) & (lanes < stop), 0.0, panel)
            update = product(right, own, (0, 0))
            below = m_ref[stop:, :]
            fresh = (columns[stop:] >= start) & (columns[stop:] < stop)
            m_ref[stop:, :] = jnp.where(fresh, 0.0, below) - update[stop:, :]


def chain_kernel(sizes, own_ref, left_ref, turned_ref, current, inverses, back_ref, sketch, packed, gathered, land0, land1, land2,
                 sum0, sum1, sum2, m_ref, send0, recv0, send1, recv1, send2, recv2, send3, recv3, send4, recv4, send5, recv5,
                 own_sem, z_send, z_recv, x_send, x_recv):
    chips, count = sizes
    n = own_ref.shape[1]
    t, f = lax.axis_index("tp"), lax.axis_index("fsdp")
    y, c = t // 2, t % 2
    z, x = f // 2, f % 2
    lines = count // 2
    stages = [
        (2, c, lambda i: {"tp": 2 * y + i}),
        (chips, y, lambda i: {"tp": 2 * i + c}),
        (count, f, lambda i: {"fsdp": i}),
    ]
    barrier = pltpu.get_barrier_semaphore()
    for members, me, device in stages:
        for step in range(1, members):
            pl.semaphore_signal(barrier, inc=1, device_id=device(lax.rem(me + step, members)), device_id_type=MESH)
    own_copy = pltpu.make_async_copy(own_ref, sketch.at[f], own_sem)
    own_copy.start()
    current[...] = own_ref[...]
    pl.semaphore_wait(barrier, sum(members - 1 for members, _, _ in stages))

    def rows(index, size):
        return pl.ds(pl.multiple_of(index * size, size), size)

    def remote(source, target, send, recv, device):
        return pltpu.make_async_remote_copy(src_ref=source, dst_ref=target, send_sem=send, recv_sem=recv,
                                            device_id=device, device_id_type=MESH)

    def exchange(stage, pick, put, send, recv):
        members, me, device = stage
        copies = []
        for step in range(1, members):
            target = lax.rem(me + step, members)
            copies.append(remote(pick(target), put(step), send.at[step], recv.at[step], device(target)))
        for copy in copies:
            copy.start()
        return copies

    along = [remote(own_ref, sketch.at[f], z_send.at[step], z_recv.at[step], {"fsdp": 2 * lax.rem(z + step, lines) + x})
             for step in range(1, lines)]
    across = [remote(sketch.at[2 * i + x], sketch.at[2 * i + x], x_send.at[i], x_recv.at[i], {"fsdp": 2 * z + 1 - x})
              for i in range(lines)]
    blocks = n // BLOCK

    def turn(r, carry):
        place = 0
        places = {}
        for i in range(blocks):
            strip = product(current[:, i * BLOCK:(i + 1) * BLOCK], current[:, i * BLOCK:], (0, 0))
            for j in range(i, blocks):
                packed[place:place + BLOCK, :] = strip[:, (j - i) * BLOCK:(j - i + 1) * BLOCK]
                places[i, j] = place
                place += BLOCK
        started = []
        source, base, size = packed, 0, place
        downs = ((land0, sum0, send0, recv0), (land1, sum1, send1, recv1), (land2, sum2, send2, recv2))
        for stage, (land, total_ref, send, recv) in zip(stages, downs):
            members, me, _ = stage
            size = size // members
            copies = exchange(stage, lambda i: source.at[rows(i, size)], lambda step: land.at[step], send, recv)
            started += copies
            total = source[rows(me, size), :]
            for step in range(1, members):
                copies[step - 1].wait_recv()
                total = total + land[step]
            total_ref[...] = total
            base = base + me * size
            source = total_ref
        gathered[pl.ds(pl.multiple_of(base, size), size), :] = total
        source = sum2
        for stage, (send, recv) in zip(stages[::-1], ((send3, recv3), (send4, recv4), (send5, recv5))):
            members, me, _ = stage
            spot = gathered.at[pl.ds(pl.multiple_of(base, size), size)]
            copies = exchange(stage, lambda i: source, lambda step: spot, send, recv)
            started += copies
            for copy in copies:
                copy.wait_recv()
            base = base - me * size
            size = size * members
            source = gathered.at[pl.ds(pl.multiple_of(base, size), size)]
        for copy in started:
            copy.wait_send()

        @pl.when(r == 0)
        def _():
            for copy in along:
                copy.start()

        @pl.when(r == 1)
        def _():
            own_copy.wait()
            for copy in along:
                copy.wait_recv()
            for copy in across:
                copy.start()

        x_ref = inverses.at[r]
        for i in range(blocks):
            for j in range(i, blocks):
                x_ref[i * BLOCK:(i + 1) * BLOCK, j * BLOCK:(j + 1) * BLOCK] = gathered[places[i, j]:places[i, j] + BLOCK, :]
        inverse_kernel(x_ref, m_ref)
        current[...] = product(current[...], x_ref[...], (1, 1))
        return carry

    lax.fori_loop(0, 2, turn, 0)
    left_ref[...] = current[...]
    back_ref[...] = product(inverses[1], inverses[0], (1, 0))
    size = own_ref.shape[0]
    for copy in across:
        copy.wait_recv()

    def multiply(i, carry):
        turned_ref[:, rows(i, size)] = product(back_ref[...], sketch[i], (1, 1))
        return carry

    lax.fori_loop(0, count, multiply, 0)
    for copy in along + across:
        copy.wait_send()


def inverse_kernel(x_ref, m_ref):
    n = x_ref.shape[0]
    for start in range(0, n, BLOCK):
        stop = start + BLOCK
        m_ref[...] = x_ref[start:stop, start:stop]
        eliminate_block(m_ref)
        diagonal = m_ref[...]
        x_ref[start:stop, start:stop] = diagonal
        if start > 0:
            x_ref[start:stop, :start] = product(diagonal, x_ref[start:stop, :start], (1, 0))
        if stop < n:
            right = product(diagonal, x_ref[start:stop, stop:], (1, 0))
            if start > 0:
                x_ref[stop:, :start] -= product(right, x_ref[start:stop, :start], (0, 0))
            x_ref[stop:, start:stop] = -product(right, diagonal, (0, 0))
            x_ref[stop:, stop:] -= product(right, right, (0, 0))
            x_ref[start:stop, stop:] = jnp.zeros((BLOCK, n - stop), jnp.float32)


def orthonormal_chain(own, chips, count):
    rows, n = own.shape
    blocks = n // BLOCK
    packed = BLOCK * blocks * (blocks + 1) // 2
    dma = pltpu.SemaphoreType.DMA
    f32 = jnp.float32
    half, part = packed // 2, packed // 2 // chips
    return pl.pallas_call(
        functools.partial(chain_kernel, (chips, count)),
        out_shape=[jax.ShapeDtypeStruct((rows, n), f32), jax.ShapeDtypeStruct((n, rows * count), f32)],
        in_specs=[pl.BlockSpec(memory_space=pltpu.VMEM)],
        out_specs=[pl.BlockSpec(memory_space=pltpu.VMEM)] * 2,
        scratch_shapes=[
            pltpu.VMEM((rows, n), f32),
            pltpu.VMEM((2, n, n), f32),
            pltpu.VMEM((n, n), f32),
            pltpu.VMEM((count, rows, n), f32),
            pltpu.VMEM((packed, BLOCK), f32),
            pltpu.VMEM((packed, BLOCK), f32),
            pltpu.VMEM((2, half, BLOCK), f32),
            pltpu.VMEM((chips, part, BLOCK), f32),
            pltpu.VMEM((count, part // count, BLOCK), f32),
            pltpu.VMEM((half, BLOCK), f32),
            pltpu.VMEM((part, BLOCK), f32),
            pltpu.VMEM((part // count, BLOCK), f32),
            pltpu.VMEM((BLOCK, BLOCK), f32),
        ] + [dma((members,)) for members in (2, 2, chips, chips, count, count, count, count, chips, chips, 2, 2)]
        + [dma] + [dma((count // 2,))] * 4,
        compiler_params=pltpu.CompilerParams(collective_id=2, has_side_effects=True, vmem_limit_bytes=40 * 1024 * 1024),
        cost_estimate=pl.CostEstimate(flops=2 * n * n * n * 40, bytes_accessed=16 * n * n, transcendentals=n),
        name="orthonormal_chain",
    )(own)


def inverse_factor(gram):
    n = gram.shape[0]

    def kernel(g_ref, x_ref, m_ref):
        x_ref[...] = g_ref[...]
        inverse_kernel(x_ref, m_ref)

    return pl.pallas_call(
        kernel,
        out_shape=jax.ShapeDtypeStruct((n, n), jnp.float32),
        in_specs=[pl.BlockSpec(memory_space=pltpu.VMEM)],
        out_specs=pl.BlockSpec(memory_space=pltpu.VMEM),
        scratch_shapes=[pltpu.VMEM((BLOCK, BLOCK), jnp.float32)],
        cost_estimate=pl.CostEstimate(flops=2 * n * n * n * 20, bytes_accessed=8 * n * n, transcendentals=n),
        name="inverse_factor",
    )(gram)


def pieces_of(value):
    high = value.astype(jnp.bfloat16)
    rest = value - high.astype(jnp.float32)
    middle = rest.astype(jnp.bfloat16)
    low = (rest - middle.astype(jnp.float32)).astype(jnp.bfloat16)
    return high, middle, low


def sketch_kernel(m_hbm, g_hbm, b_hbm, out_ref, m_buf, g_buf, land, split, part, land_x, summed, land_z,
                  m_sem, g_sem, own_sem, core_send, core_recv, y_send, y_recv, relay_send, relay_recv,
                  x_send, x_recv, z_send, z_recv):
    t, f = lax.axis_index("tp"), lax.axis_index("fsdp")
    y, c = t // 2, t % 2
    z, x = f // 2, f % 2
    width = b_hbm.shape[1]
    depth = m_hbm.shape[1]
    half = depth // 2
    block = m_hbm.shape[0] // 4
    own = block // 2
    core_peer = {"tp": 2 * y + 1 - c}
    y_peer = {"tp": 2 * (1 - y) + c}
    x_peer = {"fsdp": 2 * z + 1 - x}

    def order(j):
        return 2 * ((z // 2 + (3 - j) // 2) % 2) + (z % 2 + (3 - j) % 2) % 2

    barrier = pltpu.get_barrier_semaphore()
    for peer in [core_peer, y_peer, x_peer] + [{"fsdp": 2 * order(j) + x} for j in range(3)]:
        pl.semaphore_signal(barrier, inc=1, device_id=peer, device_id_type=MESH)

    def fetch(s):
        j = s % 4 * (s // 8) + (s // 2) * (1 - s // 8)
        k = (s % 2) * (1 - s // 8) + (s // 12)
        slot = s % 2
        rows = pl.ds(pl.multiple_of(order(j) * block, block), block)
        columns = pl.ds(pl.multiple_of(k * half, half), half)
        return (pltpu.make_async_copy(m_hbm.at[rows, columns], m_buf.at[slot], m_sem.at[slot]),
                pltpu.make_async_copy(g_hbm.at[rows, columns], g_buf.at[slot], g_sem.at[slot]))

    own_copy = pltpu.make_async_copy(b_hbm, land.at[0], own_sem)
    own_copy.start()
    for copy in fetch(0):
        copy.start()
    pl.semaphore_wait(barrier, 6)

    quarter = depth // 4

    def remote(source, target, send, recv, peer):
        return pltpu.make_async_remote_copy(src_ref=source, dst_ref=target, send_sem=send, recv_sem=recv,
                                            device_id=peer, device_id_type=MESH)

    to_core = [remote(b_hbm.at[pl.ds(k * half, half)], land.at[1, pl.ds(k * half, half)],
                      core_send.at[k], core_recv.at[k], core_peer) for k in range(2)]
    to_y = [remote(b_hbm.at[pl.ds(q * quarter, quarter)], land.at[2, pl.ds(q * quarter, quarter)],
                   y_send.at[q], y_recv.at[q], y_peer) for q in range(4)]
    relay = [remote(land.at[2, pl.ds(q * quarter, quarter)], land.at[3, pl.ds(q * quarter, quarter)],
                    relay_send.at[q], relay_recv.at[q], core_peer) for q in range(4)]
    for copy in to_core + to_y:
        copy.start()

    def cut(slot, column, k):
        columns = pl.ds(pl.multiple_of(column * width, width), width)

        def body(i, carry):
            rows = pl.ds(pl.multiple_of(k * half + i * CHUNK, CHUNK), CHUNK)
            high, middle, low = pieces_of(land[slot, rows, :])
            for place, piece in enumerate((high, middle, low, high, middle, high)):
                split[k, i, place * CHUNK:(place + 1) * CHUNK, columns] = piece
            return carry

        lax.fori_loop(0, half // CHUNK, body, 0)

    part[...] = jnp.zeros_like(part)
    own_copy.wait()
    cut(0, c, 0)
    to_core[0].wait_recv()
    cut(1, 1 - c, 0)

    across = [[remote(part.at[n, j, pl.ds(pl.multiple_of((1 - x) * own, own), own)], land_x.at[n, j],
                      x_send.at[n, j], x_recv.at[n, j], x_peer) for j in range(4)] for n in range(2)]
    along = [[remote(summed.at[n, j], land_z.at[n, j], z_send.at[n, j], z_recv.at[n, j],
                     {"fsdp": 2 * order(j) + x}) for j in range(3)] for n in range(2)]

    def add_x(n, j):
        across[n][j].wait_recv()

        def body(i, carry):
            rows = pl.ds(pl.multiple_of(i * 64, 64), 64)
            mine = pl.ds(pl.multiple_of(x * own + i * 64, 64), 64)
            summed[n, j, rows, :] = part[n, j, mine, :] + land_x[n, j, rows, :]
            return carry

        lax.fori_loop(0, own // 64, body, 0)
        if j < 3:
            along[n][j].start()

    before = {}
    after = {}

    def at(table, s, action):
        table.setdefault(s, []).append(action)

    def second_half():
        cut(0, c, 1)
        to_core[1].wait_recv()
        cut(1, 1 - c, 1)

    def pass_on(q):
        to_y[q].wait_recv()
        relay[q].start()

    def other_chip(k):
        cut(2, c, k)
        relay[2 * k].wait_recv()
        relay[2 * k + 1].wait_recv()
        cut(3, 1 - c, k)

    at(before, 1, second_half)
    at(before, 4, lambda: pass_on(0))
    at(before, 7, lambda: pass_on(1))
    at(before, 8, lambda: other_chip(0))
    at(before, 10, lambda: pass_on(2))
    at(before, 12, lambda: pass_on(3))
    at(before, 12, lambda: other_chip(1))
    for j in range(4):
        at(after, 2 * j + 1, lambda j=j: across[0][j].start())
        at(after, 2 * j + 3, lambda j=j: add_x(0, j))
        at(after, 12 + j, lambda j=j: across[1][j].start())
    at(after, 14, lambda: add_x(1, 0))
    at(after, 15, lambda: add_x(1, 1))

    def step(s, carry):
        for copy in fetch(s):
            copy.wait()

        @pl.when(s < 15)
        def _():
            for copy in fetch(s + 1):
                copy.start()

        for when, actions in before.items():
            @pl.when(s == when)
            def _(actions=actions):
                for action in actions:
                    action()

        slot = s % 2
        j = s % 4 * (s // 8) + (s // 2) * (1 - s // 8)
        k = (s % 2) * (1 - s // 8) + (s // 12)
        n = s // 8

        def body(i, inner):
            columns = pl.ds(pl.multiple_of(i * CHUNK, CHUNK), CHUNK)
            value = m_buf[slot, :, columns] + g_buf[slot, :, columns].astype(jnp.float32)
            high, middle, low = pieces_of(value)
            left = jnp.concatenate([high, high, high, middle, middle, low], axis=1)
            part[n, j] += jnp.dot(left, split[k, i], preferred_element_type=jnp.float32)
            return inner

        lax.fori_loop(0, half // CHUNK, body, 0)
        for when, actions in after.items():
            @pl.when(s == when)
            def _(actions=actions):
                for action in actions:
                    action()
        return carry

    lax.fori_loop(0, 16, step, 0)
    add_x(1, 2)
    add_x(1, 3)
    for n in range(2):
        for j in range(3):
            along[n][j].wait_recv()
        columns = pl.ds(pl.multiple_of((y * (1 - n) + (1 - y) * n) * 2 * width, 2 * width), 2 * width)
        out_ref[:, columns] = summed[n, 3] + land_z[n, 0] + land_z[n, 1] + land_z[n, 2]
    for copy in to_core + to_y + relay + across[0] + across[1] + along[0] + along[1]:
        copy.wait_send()


def sketch_rows(momentum, gradient, basis):
    rows, depth = momentum.shape
    width = basis.shape[1]
    block, half = rows // 4, depth // 2
    own = block // 2
    dma = pltpu.SemaphoreType.DMA
    f32 = jnp.float32
    return pl.pallas_call(
        sketch_kernel,
        out_shape=jax.ShapeDtypeStruct((own, 4 * width), f32),
        in_specs=[pl.BlockSpec(memory_space=pl.ANY)] * 3,
        out_specs=pl.BlockSpec(memory_space=pltpu.VMEM),
        scratch_shapes=[
            pltpu.VMEM((2, block, half), f32),
            pltpu.VMEM((2, block, half), jnp.bfloat16),
            pltpu.VMEM((4, depth, width), f32),
            pltpu.VMEM((2, half // CHUNK, 6 * CHUNK, 2 * width), jnp.bfloat16),
            pltpu.VMEM((2, 4, block, 2 * width), f32),
            pltpu.VMEM((2, 4, own, 2 * width), f32),
            pltpu.VMEM((2, 4, own, 2 * width), f32),
            pltpu.VMEM((2, 3, own, 2 * width), f32),
            dma((2,)), dma((2,)), dma, dma((2,)), dma((2,)), dma((4,)), dma((4,)), dma((4,)), dma((4,)),
            dma((2, 4)), dma((2, 4)), dma((2, 3)), dma((2, 3)),
        ],
        compiler_params=pltpu.CompilerParams(collective_id=1, has_side_effects=True, vmem_limit_bytes=60 * 1024 * 1024),
        cost_estimate=pl.CostEstimate(flops=12 * rows * depth * 4 * width, bytes_accessed=12 * rows * depth, transcendentals=0),
        name="sketch_rows",
    )(momentum, gradient, basis)


def right_kernel(count, m_hbm, g_hbm, left_ref, right_ref, basis_ref, m_buf, g_buf, high_ref, low_ref, part, land_c, summed, land_y,
                 rows_ref, squares, land_s, m_sem, g_sem, core_send, core_recv, y_send, y_recv, keep_send, keep_recv,
                 over_send, over_recv, relay_send, relay_recv, s_send, s_recv):
    t, f = lax.axis_index("tp"), lax.axis_index("fsdp")
    y, c = t // 2, t % 2
    rank, depth = left_ref.shape
    width = rank // 4
    steps = part.shape[0]
    core_peer = {"tp": 2 * y + 1 - c}
    y_peer = {"tp": 2 * (1 - y) + c}
    other = 2 * (1 - y) + c

    barrier = pltpu.get_barrier_semaphore()
    for peer in [core_peer, y_peer] + [{"fsdp": lax.rem(f + step, count)} for step in range(1, count)]:
        pl.semaphore_signal(barrier, inc=1, device_id=peer, device_id_type=MESH)

    def fetch(s):
        columns = pl.ds(pl.multiple_of(s * CHUNK, CHUNK), CHUNK)
        return (pltpu.make_async_copy(m_hbm.at[:, columns], m_buf.at[s % 2], m_sem.at[s % 2]),
                pltpu.make_async_copy(g_hbm.at[:, columns], g_buf.at[s % 2], g_sem.at[s % 2]))

    for copy in fetch(0):
        copy.start()

    def remote(source, target, send, recv, peer):
        return pltpu.make_async_remote_copy(src_ref=source, dst_ref=target, send_sem=send, recv_sem=recv,
                                            device_id=peer, device_id_type=MESH)

    def band(index):
        return pl.ds(pl.multiple_of(index * width, width), width)

    def spot(index, s):
        return right_ref.at[band(index), pl.ds(pl.multiple_of(s * CHUNK, CHUNK), CHUNK)]

    def to_core(s, chip):
        return remote(part.at[s, band(2 * chip + 1 - c)], land_c.at[s, chip], core_send.at[s, chip], core_recv.at[s, chip], core_peer)

    def to_y(s):
        return remote(summed.at[s, 1 - y], land_y.at[s], y_send.at[s], y_recv.at[s], y_peer)

    def keep(s):
        return remote(spot(t, s), spot(t, s), keep_send.at[s], keep_recv.at[s], core_peer)

    def over(s):
        return remote(spot(t, s), spot(t, s), over_send.at[s], over_recv.at[s], y_peer)

    def relay(s):
        return remote(spot(other, s), spot(other, s), relay_send.at[s], relay_recv.at[s], core_peer)

    def split(i, carry):
        columns = pl.ds(pl.multiple_of(i * CHUNK, CHUNK), CHUNK)
        value = left_ref[:, columns]
        high = value.astype(jnp.bfloat16)
        high_ref[i] = high
        low_ref[i] = (value - high.astype(jnp.float32)).astype(jnp.bfloat16)
        return carry

    lax.fori_loop(0, depth // CHUNK, split, 0)
    squares[...] = jnp.zeros_like(squares)
    pl.semaphore_wait(barrier, 1 + count)

    def step(s, carry):
        @pl.when(s < steps)
        def _():
            for copy in fetch(s):
                copy.wait()

            @pl.when(s < steps - 1)
            def _():
                for copy in fetch(s + 1):
                    copy.start()

            part[s] = jnp.zeros((rank, CHUNK), jnp.float32)

            def body(i, inner):
                rows = pl.ds(pl.multiple_of(i * CHUNK, CHUNK), CHUNK)
                value = m_buf[s % 2, rows, :] + g_buf[s % 2, rows, :].astype(jnp.float32)
                high = value.astype(jnp.bfloat16)
                low = (value - high.astype(jnp.float32)).astype(jnp.bfloat16)
                left = jnp.concatenate([high_ref[i], high_ref[i], low_ref[i]], axis=1)
                part[s] += jnp.dot(left, jnp.concatenate([high, low, high], axis=0), preferred_element_type=jnp.float32)
                return inner

            lax.fori_loop(0, depth // CHUNK, body, 0)
            for chip in range(2):
                to_core(s, chip).start()

        @pl.when((s >= 1) & (s < steps + 1))
        def _():
            now = s - 1
            for chip in range(2):
                to_core(now, chip).wait_recv()
                summed[now, chip] = part[now, band(2 * chip + c), :] + land_c[now, chip]
            to_y(now).start()

        @pl.when((s >= 4) & (s < steps + 4))
        def _():
            now = s - 4
            to_y(now).wait_recv()
            mine = summed[now, y] + land_y[now]
            right_ref[band(t), pl.ds(pl.multiple_of(now * CHUNK, CHUNK), CHUNK)] = mine
            over(now).start()
            keep(now).start()
            turned = mine.T
            rows_ref[pl.ds(pl.multiple_of(now * CHUNK, CHUNK), CHUNK), :] = turned
            squares[...] += jnp.sum((turned * turned).reshape(CHUNK // 8, 8, width), axis=0)

        @pl.when(s >= 7)
        def _():
            now = s - 7
            over(now).wait_recv()
            relay(now).start()
        return carry

    lax.fori_loop(0, steps + 4, step, 0)
    spread = [remote(squares, land_s.at[step], s_send.at[step], s_recv.at[step], {"fsdp": lax.rem(f + step, count)})
              for step in range(1, count)]
    for copy in spread:
        copy.start()
    total = squares[...]
    for step in range(1, count):
        spread[step - 1].wait_recv()
        total = total + land_s[step]
    scale = jnp.sqrt(jnp.sum(total, axis=0, keepdims=True) + tiny)

    def divide(i, carry):
        rows = pl.ds(pl.multiple_of(i * CHUNK, CHUNK), CHUNK)
        basis_ref[rows, :] = rows_ref[rows, :] / scale
        return carry

    lax.fori_loop(0, steps, divide, 0)

    def last(s, carry):
        over(s).wait_recv()
        relay(s).start()
        return carry

    lax.fori_loop(steps - 3, steps, last, 0)

    def drain(s, carry):
        for chip in range(2):
            to_core(s, chip).wait_send()
        to_y(s).wait_send()
        over(s).wait_send()
        keep(s).wait()
        relay(s).wait()
        return carry

    lax.fori_loop(0, steps, drain, 0)
    for copy in spread:
        copy.wait_send()


def right_columns(momentum, gradient, left, count):
    rows, depth = momentum.shape
    rank = left.shape[0]
    width = rank // 4
    steps = depth // CHUNK
    dma = pltpu.SemaphoreType.DMA
    f32 = jnp.float32
    return pl.pallas_call(
        functools.partial(right_kernel, count),
        out_shape=[jax.ShapeDtypeStruct((rank, depth), f32), jax.ShapeDtypeStruct((depth, width), f32)],
        in_specs=[pl.BlockSpec(memory_space=pl.ANY)] * 2 + [pl.BlockSpec(memory_space=pltpu.VMEM)],
        out_specs=[pl.BlockSpec(memory_space=pltpu.VMEM)] * 2,
        scratch_shapes=[
            pltpu.VMEM((2, rows, CHUNK), f32),
            pltpu.VMEM((2, rows, CHUNK), jnp.bfloat16),
            pltpu.VMEM((rows // CHUNK, rank, CHUNK), jnp.bfloat16),
            pltpu.VMEM((rows // CHUNK, rank, CHUNK), jnp.bfloat16),
            pltpu.VMEM((steps, rank, CHUNK), f32),
            pltpu.VMEM((steps, 2, width, CHUNK), f32),
            pltpu.VMEM((steps, 2, width, CHUNK), f32),
            pltpu.VMEM((steps, width, CHUNK), f32),
            pltpu.VMEM((depth, width), f32),
            pltpu.VMEM((8, width), f32),
            pltpu.VMEM((count, 8, width), f32),
            dma((2,)), dma((2,)), dma((steps, 2)), dma((steps, 2)), dma((steps,)), dma((steps,)), dma((steps,)), dma((steps,)),
            dma((steps,)), dma((steps,)), dma((steps,)), dma((steps,)), dma((count,)), dma((count,)),
        ],
        compiler_params=pltpu.CompilerParams(collective_id=3, has_side_effects=True, vmem_limit_bytes=60 * 1024 * 1024),
        cost_estimate=pl.CostEstimate(flops=6 * rows * depth * rank, bytes_accessed=6 * rows * depth, transcendentals=0),
        name="right_columns",
    )(momentum, gradient, left)


def sketch_own(momentum, gradient, basis, fitting):
    if fitting:
        return sketch_rows(momentum, gradient, basis)
    tile = momentum + gradient.astype(jnp.float32)
    partial_sketch = product(tile, lax.all_gather(basis, "tp", axis=1, tiled=True), (1, 0))
    return lax.psum_scatter(partial_sketch, "fsdp", scatter_dimension=0, tiled=True)


def orthonormal(own):
    inverse = inverse_factor(lax.psum(product(own, own, (0, 0)), ("fsdp", "tp")))
    return product(own, inverse, (1, 1)), inverse


def on_device(momentum, gradient, basis):
    fitting = lax.axis_size("tp") == 4 and lax.axis_size("fsdp") == 8
    own = sketch_own(momentum, gradient, basis, fitting)
    tile = momentum + gradient.astype(jnp.float32)
    if fitting:
        own_left, left = orthonormal_chain(own, lax.axis_size("tp") // 2, lax.axis_size("fsdp"))
        right, new_basis = right_columns(momentum, gradient, left, lax.axis_size("fsdp"))
        change = product(left, (1.0 - keep_rate) * right, (0, 0), lax.Precision.DEFAULT)
        return (tile - change, new_basis, own_left)
    sketch = lax.all_gather(own, "fsdp", axis=0, tiled=True)
    own_first, inverse = orthonormal(own)
    own_left, second = orthonormal(own_first)
    left = product(sketch, product(second, inverse, (1, 0)), (1, 1))
    partial_right = product(tile, left, (0, 0), lax.Precision.HIGH)
    mine = lax.psum_scatter(partial_right, "tp", scatter_dimension=1, tiled=True)
    squares = lax.psum(jnp.sum(mine * mine, axis=0), "fsdp")
    new_basis = mine / jnp.sqrt(squares + tiny)[None, :]
    full_right = lax.all_gather(mine, "tp", axis=1, tiled=True)
    new_momentum = tile - product(left, (1.0 - keep_rate) * full_right, (1, 1), lax.Precision.DEFAULT)
    return (new_momentum, new_basis, own_left)


def solution(mesh):
    placed = (P("tp", "fsdp"), P("tp", "fsdp"), P("fsdp", "tp"))
    return jax.shard_map(
        on_device,
        mesh=mesh,
        in_specs=placed,
        out_specs=(P("tp", "fsdp"), P("fsdp", "tp"), P(("tp", "fsdp"), None)),
        check_vma=False,
    )
```

```python
import functools

import jax
import jax.numpy as jnp
from jax import lax
from jax.experimental import pallas as pl
from jax.experimental.pallas import tpu as pltpu
from jax.sharding import PartitionSpec as P

keep_rate = 0.95
tiny = 1e-06
highest = lax.Precision.HIGHEST
MESH = pl.DeviceIdType.MESH
BLOCK = 128
PANEL = 32
CHUNK = 256


def product(a, b, dims, precision=highest):
    return lax.dot_general(a, b, ((dims[:1], dims[1:]), ((), ())), precision=precision, preferred_element_type=jnp.float32)


def eliminate_block(m_ref):
    lanes = lax.broadcasted_iota(jnp.int32, (8, BLOCK), 1)
    subs = lax.broadcasted_iota(jnp.int32, (8, BLOCK), 0)
    panel_lanes = lax.broadcasted_iota(jnp.int32, (PANEL, BLOCK), 1)
    panel_subs = lax.broadcasted_iota(jnp.int32, (PANEL, BLOCK), 0)
    columns = lax.broadcasted_iota(jnp.int32, (BLOCK, BLOCK), 1)
    groups = PANEL // 8

    def spread(row):
        return jnp.broadcast_to(row, (8, BLOCK))

    for start in range(0, BLOCK, PANEL):
        panel = [m_ref[start + 8 * g:start + 8 * g + 8, :] for g in range(groups)]
        heads = {(j, g): spread(panel[g][:, start + j:start + j + 1]) for j in range(PANEL) for g in range(j // 8, groups)}
        for j in range(PANEL):
            first, place = j // 8, j % 8
            pivot = spread(heads[j, first][place:place + 1, :])
            root = lax.rsqrt(pivot)
            root = root * (1.5 - (0.5 * pivot * root) * root)
            factors = {g: heads[j, g] * root for g in range(first, groups)}
            for later in range(j + 1, PANEL):
                scaled = spread(factors[later // 8][later % 8:later % 8 + 1, :])
                for g in range(later // 8, groups):
                    heads[later, g] = heads[later, g] - factors[g] * scaled
            row = jnp.where(lanes == start + j, root, spread(panel[first][place:place + 1, :]) * root)
            for g in range(first, groups):
                if g == first:
                    below = subs > place
                    kept = jnp.where((lanes == start + j) & below, 0.0, panel[g])
                    panel[g] = jnp.where(subs == place, row, kept - jnp.where(below, factors[g], 0.0) * row)
                else:
                    panel[g] = jnp.where(lanes == start + j, 0.0, panel[g]) - factors[g] * row
        whole = jnp.concatenate(panel, axis=0)
        m_ref[start:start + PANEL, :] = jnp.where(panel_lanes > start + panel_subs, 0.0, whole)
        stop = start + PANEL
        if stop < BLOCK:
            right = jnp.where(panel_lanes >= stop, whole, 0.0)
            own = jnp.where((panel_lanes > start + panel_subs) & (panel_lanes < stop), 0.0, whole)
            update = product(right, own, (0, 0))
            below = m_ref[stop:, :]
            fresh = (columns[stop:] >= start) & (columns[stop:] < stop)
            m_ref[stop:, :] = jnp.where(fresh, 0.0, below) - update[stop:, :]


def chain_kernel(sizes, own_ref, left_ref, turned_ref, current, inverses, back_ref, sketch, packed, gathered, land0, land1, land2,
                 sum0, sum1, sum2, m_ref, send0, recv0, send1, recv1, send2, recv2, send3, recv3, send4, recv4, send5, recv5,
                 own_sem, z_send, z_recv, x_send, x_recv):
    chips, count = sizes
    n = own_ref.shape[1]
    t, f = lax.axis_index("tp"), lax.axis_index("fsdp")
    y, c = t // 2, t % 2
    z, x = f // 2, f % 2
    lines = count // 2
    stages = [
        (2, c, lambda i: {"tp": 2 * y + i}),
        (chips, y, lambda i: {"tp": 2 * i + c}),
        (count, f, lambda i: {"fsdp": i}),
    ]
    barrier = pltpu.get_barrier_semaphore()
    for members, me, device in stages:
        for step in range(1, members):
            pl.semaphore_signal(barrier, inc=1, device_id=device(lax.rem(me + step, members)), device_id_type=MESH)
    own_copy = pltpu.make_async_copy(own_ref, sketch.at[f], own_sem)
    own_copy.start()
    current[...] = own_ref[...]
    pl.semaphore_wait(barrier, sum(members - 1 for members, _, _ in stages))

    def rows(index, size):
        return pl.ds(pl.multiple_of(index * size, size), size)

    def remote(source, target, send, recv, device):
        return pltpu.make_async_remote_copy(src_ref=source, dst_ref=target, send_sem=send, recv_sem=recv,
                                            device_id=device, device_id_type=MESH)

    def exchange(stage, pick, put, send, recv):
        members, me, device = stage
        copies = []
        for step in range(1, members):
            target = lax.rem(me + step, members)
            copies.append(remote(pick(target), put(step), send.at[step], recv.at[step], device(target)))
        for copy in copies:
            copy.start()
        return copies

    along = [remote(own_ref, sketch.at[f], z_send.at[step], z_recv.at[step], {"fsdp": 2 * lax.rem(z + step, lines) + x})
             for step in range(1, lines)]
    first = [remote(own_ref, sketch.at[f], x_send.at[0], x_recv.at[0], {"fsdp": 2 * z + 1 - x})]
    across = [remote(sketch.at[2 * lax.rem(z + i, lines) + x], sketch.at[2 * lax.rem(z + i, lines) + x], x_send.at[i], x_recv.at[i],
                     {"fsdp": 2 * z + 1 - x}) for i in range(1, lines)]
    blocks = n // BLOCK

    def ship(r):
        @pl.when(r == 0)
        def _():
            for copy in along + first:
                copy.start()

        @pl.when(r == 1)
        def _():
            own_copy.wait()
            for copy in along:
                copy.wait_recv()
            for copy in across:
                copy.start()

    def turn(r, carry):
        place = 0
        places = {}
        for i in range(blocks):
            strip = product(current[:, i * BLOCK:(i + 1) * BLOCK], current[:, i * BLOCK:], (0, 0))
            for j in range(i, blocks):
                packed[place:place + BLOCK, :] = strip[:, (j - i) * BLOCK:(j - i + 1) * BLOCK]
                places[i, j] = place
                place += BLOCK
        started = []
        source, base, size = packed, 0, place
        downs = ((land0, sum0, send0, recv0), (land1, sum1, send1, recv1), (land2, sum2, send2, recv2))
        for stage, (land, total_ref, send, recv) in zip(stages, downs):
            members, me, _ = stage
            size = size // members
            copies = exchange(stage, lambda i: source.at[rows(i, size)], lambda step: land.at[step], send, recv)
            started += copies
            total = source[rows(me, size), :]
            for step in range(1, members):
                copies[step - 1].wait_recv()
                total = total + land[step]
            total_ref[...] = total
            base = base + me * size
            source = total_ref
        gathered[pl.ds(pl.multiple_of(base, size), size), :] = total
        source = sum2
        for stage, (send, recv) in zip(stages[::-1], ((send3, recv3), (send4, recv4), (send5, recv5))):
            members, me, _ = stage
            spot = gathered.at[pl.ds(pl.multiple_of(base, size), size)]
            copies = exchange(stage, lambda i: source, lambda step: spot, send, recv)
            started += copies
            for copy in copies:
                copy.wait_recv()
            if members == count:
                ship(r)
            base = base - me * size
            size = size * members
            source = gathered.at[pl.ds(pl.multiple_of(base, size), size)]
        for copy in started:
            copy.wait_send()

        x_ref = inverses.at[r]
        for i in range(blocks):
            for j in range(i, blocks):
                x_ref[i * BLOCK:(i + 1) * BLOCK, j * BLOCK:(j + 1) * BLOCK] = gathered[places[i, j]:places[i, j] + BLOCK, :]
        inverse_kernel(x_ref, m_ref)
        current[...] = product(current[...], x_ref[...], (1, 1))
        return carry

    lax.fori_loop(0, 2, turn, 0)
    left_ref[...] = current[...]
    back_ref[...] = product(inverses[1], inverses[0], (1, 0))
    size = own_ref.shape[0]

    def multiply(side):
        def body(i, carry):
            turned_ref[:, rows(2 * i + side, size)] = product(back_ref[...], sketch[2 * i + side], (1, 1))
            return carry

        lax.fori_loop(0, lines, body, 0)

    multiply(x)
    for copy in first + across:
        copy.wait_recv()
    multiply(1 - x)
    for copy in along + first + across:
        copy.wait_send()


def inverse_kernel(x_ref, m_ref):
    n = x_ref.shape[0]
    for start in range(0, n, BLOCK):
        stop = start + BLOCK
        m_ref[...] = x_ref[start:stop, start:stop]
        eliminate_block(m_ref)
        diagonal = m_ref[...]
        x_ref[start:stop, start:stop] = diagonal
        if start > 0:
            x_ref[start:stop, :start] = product(diagonal, x_ref[start:stop, :start], (1, 0))
        if stop < n:
            right = product(diagonal, x_ref[start:stop, stop:], (1, 0))
            if start > 0:
                x_ref[stop:, :start] -= product(right, x_ref[start:stop, :start], (0, 0))
            x_ref[stop:, start:stop] = -product(right, diagonal, (0, 0))
            x_ref[stop:, stop:] -= product(right, right, (0, 0))
            x_ref[start:stop, stop:] = jnp.zeros((BLOCK, n - stop), jnp.float32)


def orthonormal_chain(own, chips, count):
    rows, n = own.shape
    blocks = n // BLOCK
    packed = BLOCK * blocks * (blocks + 1) // 2
    dma = pltpu.SemaphoreType.DMA
    f32 = jnp.float32
    half, part = packed // 2, packed // 2 // chips
    return pl.pallas_call(
        functools.partial(chain_kernel, (chips, count)),
        out_shape=[jax.ShapeDtypeStruct((rows, n), f32), jax.ShapeDtypeStruct((n, rows * count), f32)],
        in_specs=[pl.BlockSpec(memory_space=pltpu.VMEM)],
        out_specs=[pl.BlockSpec(memory_space=pltpu.VMEM)] * 2,
        scratch_shapes=[
            pltpu.VMEM((rows, n), f32),
            pltpu.VMEM((2, n, n), f32),
            pltpu.VMEM((n, n), f32),
            pltpu.VMEM((count, rows, n), f32),
            pltpu.VMEM((packed, BLOCK), f32),
            pltpu.VMEM((packed, BLOCK), f32),
            pltpu.VMEM((2, half, BLOCK), f32),
            pltpu.VMEM((chips, part, BLOCK), f32),
            pltpu.VMEM((count, part // count, BLOCK), f32),
            pltpu.VMEM((half, BLOCK), f32),
            pltpu.VMEM((part, BLOCK), f32),
            pltpu.VMEM((part // count, BLOCK), f32),
            pltpu.VMEM((BLOCK, BLOCK), f32),
        ] + [dma((members,)) for members in (2, 2, chips, chips, count, count, count, count, chips, chips, 2, 2)]
        + [dma] + [dma((count // 2,))] * 4,
        compiler_params=pltpu.CompilerParams(collective_id=2, has_side_effects=True, vmem_limit_bytes=40 * 1024 * 1024),
        cost_estimate=pl.CostEstimate(flops=2 * n * n * n * 40, bytes_accessed=16 * n * n, transcendentals=n),
        name="orthonormal_chain",
    )(own)


def inverse_factor(gram):
    n = gram.shape[0]

    def kernel(g_ref, x_ref, m_ref):
        x_ref[...] = g_ref[...]
        inverse_kernel(x_ref, m_ref)

    return pl.pallas_call(
        kernel,
        out_shape=jax.ShapeDtypeStruct((n, n), jnp.float32),
        in_specs=[pl.BlockSpec(memory_space=pltpu.VMEM)],
        out_specs=pl.BlockSpec(memory_space=pltpu.VMEM),
        scratch_shapes=[pltpu.VMEM((BLOCK, BLOCK), jnp.float32)],
        cost_estimate=pl.CostEstimate(flops=2 * n * n * n * 20, bytes_accessed=8 * n * n, transcendentals=n),
        name="inverse_factor",
    )(gram)


def pieces_of(value):
    high = value.astype(jnp.bfloat16)
    rest = value - high.astype(jnp.float32)
    middle = rest.astype(jnp.bfloat16)
    low = (rest - middle.astype(jnp.float32)).astype(jnp.bfloat16)
    return high, middle, low


def sketch_kernel(m_hbm, g_hbm, b_hbm, out_ref, m_buf, g_buf, land, split, part, land_x, summed, land_z,
                  m_sem, g_sem, own_sem, core_send, core_recv, y_send, y_recv, relay_send, relay_recv,
                  x_send, x_recv, z_send, z_recv):
    t, f = lax.axis_index("tp"), lax.axis_index("fsdp")
    y, c = t // 2, t % 2
    z, x = f // 2, f % 2
    width = b_hbm.shape[1]
    depth = m_hbm.shape[1]
    half = depth // 2
    block = m_hbm.shape[0] // 4
    own = block // 2
    core_peer = {"tp": 2 * y + 1 - c}
    y_peer = {"tp": 2 * (1 - y) + c}
    x_peer = {"fsdp": 2 * z + 1 - x}

    def order(j):
        return 2 * ((z // 2 + (3 - j) // 2) % 2) + (z % 2 + (3 - j) % 2) % 2

    barrier = pltpu.get_barrier_semaphore()
    for peer in [core_peer, y_peer, x_peer] + [{"fsdp": 2 * order(j) + x} for j in range(3)]:
        pl.semaphore_signal(barrier, inc=1, device_id=peer, device_id_type=MESH)

    def fetch(s):
        j = s % 4 * (s // 8) + (s // 2) * (1 - s // 8)
        k = (s % 2) * (1 - s // 8) + (s // 12)
        slot = s % 2
        rows = pl.ds(pl.multiple_of(order(j) * block, block), block)
        columns = pl.ds(pl.multiple_of(k * half, half), half)
        return (pltpu.make_async_copy(m_hbm.at[rows, columns], m_buf.at[slot], m_sem.at[slot]),
                pltpu.make_async_copy(g_hbm.at[rows, columns], g_buf.at[slot], g_sem.at[slot]))

    own_copy = pltpu.make_async_copy(b_hbm, land.at[0], own_sem)
    own_copy.start()
    for copy in fetch(0):
        copy.start()
    pl.semaphore_wait(barrier, 6)

    quarter = depth // 4

    def remote(source, target, send, recv, peer):
        return pltpu.make_async_remote_copy(src_ref=source, dst_ref=target, send_sem=send, recv_sem=recv,
                                            device_id=peer, device_id_type=MESH)

    to_core = [remote(b_hbm.at[pl.ds(k * half, half)], land.at[1, pl.ds(k * half, half)],
                      core_send.at[k], core_recv.at[k], core_peer) for k in range(2)]
    to_y = [remote(b_hbm.at[pl.ds(q * quarter, quarter)], land.at[2, pl.ds(q * quarter, quarter)],
                   y_send.at[q], y_recv.at[q], y_peer) for q in range(4)]
    relay = [remote(land.at[2, pl.ds(q * quarter, quarter)], land.at[3, pl.ds(q * quarter, quarter)],
                    relay_send.at[q], relay_recv.at[q], core_peer) for q in range(4)]
    for copy in to_core + to_y:
        copy.start()

    def cut(slot, column, k):
        columns = pl.ds(pl.multiple_of(column * width, width), width)

        def body(i, carry):
            rows = pl.ds(pl.multiple_of(k * half + i * CHUNK, CHUNK), CHUNK)
            high, middle, low = pieces_of(land[slot, rows, :])
            for place, piece in enumerate((high, middle, low, high, middle, high)):
                split[k, i, place * CHUNK:(place + 1) * CHUNK, columns] = piece
            return carry

        lax.fori_loop(0, half // CHUNK, body, 0)

    part[...] = jnp.zeros_like(part)
    own_copy.wait()
    cut(0, c, 0)
    to_core[0].wait_recv()
    cut(1, 1 - c, 0)

    across = [[remote(part.at[n, j, pl.ds(pl.multiple_of((1 - x) * own, own), own)], land_x.at[n, j],
                      x_send.at[n, j], x_recv.at[n, j], x_peer) for j in range(4)] for n in range(2)]
    along = [[remote(summed.at[n, j], land_z.at[n, j], z_send.at[n, j], z_recv.at[n, j],
                     {"fsdp": 2 * order(j) + x}) for j in range(3)] for n in range(2)]

    def add_x(n, j):
        across[n][j].wait_recv()

        def body(i, carry):
            rows = pl.ds(pl.multiple_of(i * 64, 64), 64)
            mine = pl.ds(pl.multiple_of(x * own + i * 64, 64), 64)
            summed[n, j, rows, :] = part[n, j, mine, :] + land_x[n, j, rows, :]
            return carry

        lax.fori_loop(0, own // 64, body, 0)
        if j < 3:
            along[n][j].start()

    before = {}
    after = {}

    def at(table, s, action):
        table.setdefault(s, []).append(action)

    def second_half():
        cut(0, c, 1)
        to_core[1].wait_recv()
        cut(1, 1 - c, 1)

    def pass_on(q):
        to_y[q].wait_recv()
        relay[q].start()

    def other_chip(k):
        cut(2, c, k)
        relay[2 * k].wait_recv()
        relay[2 * k + 1].wait_recv()
        cut(3, 1 - c, k)

    at(before, 1, second_half)
    at(before, 4, lambda: pass_on(0))
    at(before, 7, lambda: pass_on(1))
    at(before, 8, lambda: other_chip(0))
    at(before, 10, lambda: pass_on(2))
    at(before, 12, lambda: pass_on(3))
    at(before, 12, lambda: other_chip(1))
    for j in range(4):
        at(after, 2 * j + 1, lambda j=j: across[0][j].start())
        at(after, 2 * j + 3, lambda j=j: add_x(0, j))
        at(after, 12 + j, lambda j=j: across[1][j].start())
    at(after, 14, lambda: add_x(1, 0))
    at(after, 15, lambda: add_x(1, 1))

    def step(s, carry):
        for copy in fetch(s):
            copy.wait()

        @pl.when(s < 15)
        def _():
            for copy in fetch(s + 1):
                copy.start()

        for when, actions in before.items():
            @pl.when(s == when)
            def _(actions=actions):
                for action in actions:
                    action()

        slot = s % 2
        j = s % 4 * (s // 8) + (s // 2) * (1 - s // 8)
        k = (s % 2) * (1 - s // 8) + (s // 12)
        n = s // 8

        def body(i, inner):
            columns = pl.ds(pl.multiple_of(i * CHUNK, CHUNK), CHUNK)
            value = m_buf[slot, :, columns] + g_buf[slot, :, columns].astype(jnp.float32)
            high, middle, low = pieces_of(value)
            left = jnp.concatenate([high, high, high, middle, middle, low], axis=1)
            part[n, j] += jnp.dot(left, split[k, i], preferred_element_type=jnp.float32)
            return inner

        lax.fori_loop(0, half // CHUNK, body, 0, unroll=True)
        for when, actions in after.items():
            @pl.when(s == when)
            def _(actions=actions):
                for action in actions:
                    action()
        return carry

    lax.fori_loop(0, 16, step, 0)
    add_x(1, 2)
    add_x(1, 3)
    for n in range(2):
        for j in range(3):
            along[n][j].wait_recv()
        columns = pl.ds(pl.multiple_of((y * (1 - n) + (1 - y) * n) * 2 * width, 2 * width), 2 * width)
        out_ref[:, columns] = summed[n, 3] + land_z[n, 0] + land_z[n, 1] + land_z[n, 2]
    for copy in to_core + to_y + relay + across[0] + across[1] + along[0] + along[1]:
        copy.wait_send()


def sketch_rows(momentum, gradient, basis):
    rows, depth = momentum.shape
    width = basis.shape[1]
    block, half = rows // 4, depth // 2
    own = block // 2
    dma = pltpu.SemaphoreType.DMA
    f32 = jnp.float32
    return pl.pallas_call(
        sketch_kernel,
        out_shape=jax.ShapeDtypeStruct((own, 4 * width), f32),
        in_specs=[pl.BlockSpec(memory_space=pl.ANY)] * 3,
        out_specs=pl.BlockSpec(memory_space=pltpu.VMEM),
        scratch_shapes=[
            pltpu.VMEM((2, block, half), f32),
            pltpu.VMEM((2, block, half), jnp.bfloat16),
            pltpu.VMEM((4, depth, width), f32),
            pltpu.VMEM((2, half // CHUNK, 6 * CHUNK, 2 * width), jnp.bfloat16),
            pltpu.VMEM((2, 4, block, 2 * width), f32),
            pltpu.VMEM((2, 4, own, 2 * width), f32),
            pltpu.VMEM((2, 4, own, 2 * width), f32),
            pltpu.VMEM((2, 3, own, 2 * width), f32),
            dma((2,)), dma((2,)), dma, dma((2,)), dma((2,)), dma((4,)), dma((4,)), dma((4,)), dma((4,)),
            dma((2, 4)), dma((2, 4)), dma((2, 3)), dma((2, 3)),
        ],
        compiler_params=pltpu.CompilerParams(collective_id=1, has_side_effects=True, vmem_limit_bytes=60 * 1024 * 1024),
        cost_estimate=pl.CostEstimate(flops=12 * rows * depth * 4 * width, bytes_accessed=12 * rows * depth, transcendentals=0),
        name="sketch_rows",
    )(momentum, gradient, basis)


def right_kernel(count, m_hbm, g_hbm, left_ref, right_ref, basis_ref, m_buf, g_buf, high_ref, low_ref, part, land_c, summed, land_y,
                 rows_ref, squares, land_s, m_sem, g_sem, core_send, core_recv, y_send, y_recv, keep_send, keep_recv,
                 over_send, over_recv, relay_send, relay_recv, s_send, s_recv):
    t, f = lax.axis_index("tp"), lax.axis_index("fsdp")
    y, c = t // 2, t % 2
    rank, depth = left_ref.shape
    width = rank // 4
    steps = part.shape[0]
    core_peer = {"tp": 2 * y + 1 - c}
    y_peer = {"tp": 2 * (1 - y) + c}
    other = 2 * (1 - y) + c

    barrier = pltpu.get_barrier_semaphore()
    for peer in [core_peer, y_peer] + [{"fsdp": lax.rem(f + step, count)} for step in range(1, count)]:
        pl.semaphore_signal(barrier, inc=1, device_id=peer, device_id_type=MESH)

    def fetch(s):
        columns = pl.ds(pl.multiple_of(s * CHUNK, CHUNK), CHUNK)
        return (pltpu.make_async_copy(m_hbm.at[:, columns], m_buf.at[s % 2], m_sem.at[s % 2]),
                pltpu.make_async_copy(g_hbm.at[:, columns], g_buf.at[s % 2], g_sem.at[s % 2]))

    for copy in fetch(0):
        copy.start()

    def remote(source, target, send, recv, peer):
        return pltpu.make_async_remote_copy(src_ref=source, dst_ref=target, send_sem=send, recv_sem=recv,
                                            device_id=peer, device_id_type=MESH)

    def band(index):
        return pl.ds(pl.multiple_of(index * width, width), width)

    def spot(index, s):
        return right_ref.at[band(index), pl.ds(pl.multiple_of(s * CHUNK, CHUNK), CHUNK)]

    def to_core(s, chip):
        return remote(part.at[s, band(2 * chip + 1 - c)], land_c.at[s, chip], core_send.at[s, chip], core_recv.at[s, chip], core_peer)

    def to_y(s):
        return remote(summed.at[s, 1 - y], land_y.at[s], y_send.at[s], y_recv.at[s], y_peer)

    def keep(s):
        return remote(spot(t, s), spot(t, s), keep_send.at[s], keep_recv.at[s], core_peer)

    def over(s):
        return remote(spot(t, s), spot(t, s), over_send.at[s], over_recv.at[s], y_peer)

    def relay(s):
        return remote(spot(other, s), spot(other, s), relay_send.at[s], relay_recv.at[s], core_peer)

    def split(i, carry):
        columns = pl.ds(pl.multiple_of(i * CHUNK, CHUNK), CHUNK)
        value = left_ref[:, columns]
        high = value.astype(jnp.bfloat16)
        high_ref[i] = high
        low_ref[i] = (value - high.astype(jnp.float32)).astype(jnp.bfloat16)
        return carry

    lax.fori_loop(0, depth // CHUNK, split, 0)
    squares[...] = jnp.zeros_like(squares)
    pl.semaphore_wait(barrier, 1 + count)

    def step(s, carry):
        @pl.when(s < steps)
        def _():
            for copy in fetch(s):
                copy.wait()

            @pl.when(s < steps - 1)
            def _():
                for copy in fetch(s + 1):
                    copy.start()

            part[s] = jnp.zeros((rank, CHUNK), jnp.float32)

            def body(i, inner):
                rows = pl.ds(pl.multiple_of(i * CHUNK, CHUNK), CHUNK)
                value = m_buf[s % 2, rows, :] + g_buf[s % 2, rows, :].astype(jnp.float32)
                high = value.astype(jnp.bfloat16)
                low = (value - high.astype(jnp.float32)).astype(jnp.bfloat16)
                left = jnp.concatenate([high_ref[i], high_ref[i], low_ref[i]], axis=1)
                part[s] += jnp.dot(left, jnp.concatenate([high, low, high], axis=0), preferred_element_type=jnp.float32)
                return inner

            lax.fori_loop(0, depth // CHUNK, body, 0, unroll=True)
            for chip in range(2):
                to_core(s, chip).start()

        @pl.when((s >= 1) & (s < steps + 1))
        def _():
            now = s - 1
            for chip in range(2):
                to_core(now, chip).wait_recv()
                summed[now, chip] = part[now, band(2 * chip + c), :] + land_c[now, chip]
            to_y(now).start()

        @pl.when((s >= 4) & (s < steps + 4))
        def _():
            now = s - 4
            to_y(now).wait_recv()
            mine = summed[now, y] + land_y[now]
            right_ref[band(t), pl.ds(pl.multiple_of(now * CHUNK, CHUNK), CHUNK)] = mine
            over(now).start()
            keep(now).start()
            turned = mine.T
            rows_ref[pl.ds(pl.multiple_of(now * CHUNK, CHUNK), CHUNK), :] = turned
            squares[...] += jnp.sum((turned * turned).reshape(CHUNK // 8, 8, width), axis=0)

        @pl.when(s >= 7)
        def _():
            now = s - 7
            over(now).wait_recv()
            relay(now).start()
        return carry

    lax.fori_loop(0, steps + 4, step, 0)
    spread = [remote(squares, land_s.at[step], s_send.at[step], s_recv.at[step], {"fsdp": lax.rem(f + step, count)})
              for step in range(1, count)]
    for copy in spread:
        copy.start()
    total = squares[...]
    for step in range(1, count):
        spread[step - 1].wait_recv()
        total = total + land_s[step]
    scale = jnp.sqrt(jnp.sum(total, axis=0, keepdims=True) + tiny)

    def divide(i, carry):
        rows = pl.ds(pl.multiple_of(i * CHUNK, CHUNK), CHUNK)
        basis_ref[rows, :] = rows_ref[rows, :] / scale
        return carry

    lax.fori_loop(0, steps, divide, 0)

    def last(s, carry):
        over(s).wait_recv()
        relay(s).start()
        return carry

    lax.fori_loop(steps - 3, steps, last, 0)

    def drain(s, carry):
        for chip in range(2):
            to_core(s, chip).wait_send()
        to_y(s).wait_send()
        over(s).wait_send()
        keep(s).wait()
        relay(s).wait()
        return carry

    lax.fori_loop(0, steps, drain, 0)
    for copy in spread:
        copy.wait_send()


def right_columns(momentum, gradient, left, count):
    rows, depth = momentum.shape
    rank = left.shape[0]
    width = rank // 4
    steps = depth // CHUNK
    dma = pltpu.SemaphoreType.DMA
    f32 = jnp.float32
    return pl.pallas_call(
        functools.partial(right_kernel, count),
        out_shape=[jax.ShapeDtypeStruct((rank, depth), f32), jax.ShapeDtypeStruct((depth, width), f32)],
        in_specs=[pl.BlockSpec(memory_space=pl.ANY)] * 2 + [pl.BlockSpec(memory_space=pltpu.VMEM)],
        out_specs=[pl.BlockSpec(memory_space=pltpu.VMEM)] * 2,
        scratch_shapes=[
            pltpu.VMEM((2, rows, CHUNK), f32),
            pltpu.VMEM((2, rows, CHUNK), jnp.bfloat16),
            pltpu.VMEM((rows // CHUNK, rank, CHUNK), jnp.bfloat16),
            pltpu.VMEM((rows // CHUNK, rank, CHUNK), jnp.bfloat16),
            pltpu.VMEM((steps, rank, CHUNK), f32),
            pltpu.VMEM((steps, 2, width, CHUNK), f32),
            pltpu.VMEM((steps, 2, width, CHUNK), f32),
            pltpu.VMEM((steps, width, CHUNK), f32),
            pltpu.VMEM((depth, width), f32),
            pltpu.VMEM((8, width), f32),
            pltpu.VMEM((count, 8, width), f32),
            dma((2,)), dma((2,)), dma((steps, 2)), dma((steps, 2)), dma((steps,)), dma((steps,)), dma((steps,)), dma((steps,)),
            dma((steps,)), dma((steps,)), dma((steps,)), dma((steps,)), dma((count,)), dma((count,)),
        ],
        compiler_params=pltpu.CompilerParams(collective_id=3, has_side_effects=True, vmem_limit_bytes=60 * 1024 * 1024),
        cost_estimate=pl.CostEstimate(flops=6 * rows * depth * rank, bytes_accessed=6 * rows * depth, transcendentals=0),
        name="right_columns",
    )(momentum, gradient, left)


def sketch_own(momentum, gradient, basis, fitting):
    if fitting:
        return sketch_rows(momentum, gradient, basis)
    tile = momentum + gradient.astype(jnp.float32)
    partial_sketch = product(tile, lax.all_gather(basis, "tp", axis=1, tiled=True), (1, 0))
    return lax.psum_scatter(partial_sketch, "fsdp", scatter_dimension=0, tiled=True)


def orthonormal(own):
    inverse = inverse_factor(lax.psum(product(own, own, (0, 0)), ("fsdp", "tp")))
    return product(own, inverse, (1, 1)), inverse


def on_device(momentum, gradient, basis):
    fitting = lax.axis_size("tp") == 4 and lax.axis_size("fsdp") == 8
    own = sketch_own(momentum, gradient, basis, fitting)
    if fitting:
        own_left, left = orthonormal_chain(own, lax.axis_size("tp") // 2, lax.axis_size("fsdp"))
        right, new_basis = right_columns(momentum, gradient, left, lax.axis_size("fsdp"))
        change = product(left, (1.0 - keep_rate) * right, (0, 0), lax.Precision.DEFAULT)
        return (momentum + gradient.astype(jnp.float32) - change, new_basis, own_left)
    tile = momentum + gradient.astype(jnp.float32)
    sketch = lax.all_gather(own, "fsdp", axis=0, tiled=True)
    own_first, inverse = orthonormal(own)
    own_left, second = orthonormal(own_first)
    left = product(sketch, product(second, inverse, (1, 0)), (1, 1))
    partial_right = product(tile, left, (0, 0), lax.Precision.HIGH)
    mine = lax.psum_scatter(partial_right, "tp", scatter_dimension=1, tiled=True)
    squares = lax.psum(jnp.sum(mine * mine, axis=0), "fsdp")
    new_basis = mine / jnp.sqrt(squares + tiny)[None, :]
    full_right = lax.all_gather(mine, "tp", axis=1, tiled=True)
    new_momentum = tile - product(left, (1.0 - keep_rate) * full_right, (1, 1), lax.Precision.DEFAULT)
    return (new_momentum, new_basis, own_left)


def solution(mesh):
    placed = (P("tp", "fsdp"), P("tp", "fsdp"), P("fsdp", "tp"))
    return jax.shard_map(
        on_device,
        mesh=mesh,
        in_specs=placed,
        out_specs=(P("tp", "fsdp"), P("fsdp", "tp"), P(("tp", "fsdp"), None)),
        check_vma=False,
    )
```

```python
import functools

import jax
import jax.numpy as jnp
from jax import lax
from jax.experimental import pallas as pl
from jax.experimental.pallas import tpu as pltpu
from jax.sharding import PartitionSpec as P

keep_rate = 0.95
tiny = 1e-06
highest = lax.Precision.HIGHEST
MESH = pl.DeviceIdType.MESH
BLOCK = 128
PANEL = 32
CHUNK = 256


def product(a, b, dims, precision=highest):
    return lax.dot_general(a, b, ((dims[:1], dims[1:]), ((), ())), precision=precision, preferred_element_type=jnp.float32)


def eliminate_block(m_ref):
    lanes = lax.broadcasted_iota(jnp.int32, (8, BLOCK), 1)
    subs = lax.broadcasted_iota(jnp.int32, (8, BLOCK), 0)
    panel_lanes = lax.broadcasted_iota(jnp.int32, (PANEL, BLOCK), 1)
    panel_subs = lax.broadcasted_iota(jnp.int32, (PANEL, BLOCK), 0)
    columns = lax.broadcasted_iota(jnp.int32, (BLOCK, BLOCK), 1)
    groups = PANEL // 8

    def spread(row):
        return jnp.broadcast_to(row, (8, BLOCK))

    for start in range(0, BLOCK, PANEL):
        panel = [m_ref[start + 8 * g:start + 8 * g + 8, :] for g in range(groups)]
        heads = {(j, g): spread(panel[g][:, start + j:start + j + 1]) for j in range(PANEL) for g in range(j // 8, groups)}
        for j in range(PANEL):
            first, place = j // 8, j % 8
            pivot = spread(heads[j, first][place:place + 1, :])
            root = lax.rsqrt(pivot)
            root = root * (1.5 - (0.5 * pivot * root) * root)
            factors = {g: heads[j, g] * root for g in range(first, groups)}
            for later in range(j + 1, PANEL):
                scaled = spread(factors[later // 8][later % 8:later % 8 + 1, :])
                for g in range(later // 8, groups):
                    heads[later, g] = heads[later, g] - factors[g] * scaled
            row = jnp.where(lanes == start + j, root, spread(panel[first][place:place + 1, :]) * root)
            for g in range(first, groups):
                if g == first:
                    below = subs > place
                    kept = jnp.where((lanes == start + j) & below, 0.0, panel[g])
                    panel[g] = jnp.where(subs == place, row, kept - jnp.where(below, factors[g], 0.0) * row)
                else:
                    panel[g] = jnp.where(lanes == start + j, 0.0, panel[g]) - factors[g] * row
        whole = jnp.concatenate(panel, axis=0)
        m_ref[start:start + PANEL, :] = jnp.where(panel_lanes > start + panel_subs, 0.0, whole)
        stop = start + PANEL
        if stop < BLOCK:
            right = jnp.where(panel_lanes >= stop, whole, 0.0)
            own = jnp.where((panel_lanes > start + panel_subs) & (panel_lanes < stop), 0.0, whole)
            update = product(right, own, (0, 0))
            below = m_ref[stop:, :]
            fresh = (columns[stop:] >= start) & (columns[stop:] < stop)
            m_ref[stop:, :] = jnp.where(fresh, 0.0, below) - update[stop:, :]


def chain_kernel(sizes, own_ref, left_ref, turned_ref, current, inverses, back_ref, sketch, packed, gathered, land0, land1, land2,
                 sum0, sum1, sum2, m_ref, send0, recv0, send1, recv1, send2, recv2, send3, recv3, send4, recv4, send5, recv5,
                 own_sem, z_send, z_recv, x_send, x_recv, late_send, late_recv):
    chips, count = sizes
    n = own_ref.shape[1]
    t, f = lax.axis_index("tp"), lax.axis_index("fsdp")
    y, c = t // 2, t % 2
    z, x = f // 2, f % 2
    lines = count // 2
    stages = [
        (2, c, lambda i: {"tp": 2 * y + i}),
        (chips, y, lambda i: {"tp": 2 * i + c}),
        (count, f, lambda i: {"fsdp": i}),
    ]
    barrier = pltpu.get_barrier_semaphore()
    for members, me, device in stages:
        for step in range(1, members):
            pl.semaphore_signal(barrier, inc=1, device_id=device(lax.rem(me + step, members)), device_id_type=MESH)
    own_copy = pltpu.make_async_copy(own_ref, sketch.at[f], own_sem)
    own_copy.start()
    current[...] = own_ref[...]
    pl.semaphore_wait(barrier, sum(members - 1 for members, _, _ in stages))

    def rows(index, size):
        return pl.ds(pl.multiple_of(index * size, size), size)

    def remote(source, target, send, recv, device):
        return pltpu.make_async_remote_copy(src_ref=source, dst_ref=target, send_sem=send, recv_sem=recv,
                                            device_id=device, device_id_type=MESH)

    def exchange(stage, pick, put, send, recv):
        members, me, device = stage
        copies = []
        for step in range(1, members):
            target = lax.rem(me + step, members)
            copies.append(remote(pick(target), put(step), send.at[step], recv.at[step], device(target)))
        for copy in copies:
            copy.start()
        return copies

    split = n - BLOCK
    early, late = pl.ds(0, split), pl.ds(split, BLOCK)
    mate = 2 * z + 1 - x

    def line(step):
        return {"fsdp": 2 * lax.rem(z + step, lines) + x}

    along = [remote(own_ref.at[:, early], sketch.at[f, :, early], z_send.at[step], z_recv.at[step], line(step))
             for step in range(1, lines)]
    first = [remote(own_ref, sketch.at[f], x_send.at[0], x_recv.at[0], {"fsdp": mate})]
    across = []
    for i in range(1, lines):
        spot = sketch.at[2 * lax.rem(z + i, lines) + x, :, early]
        across.append(remote(spot, spot, x_send.at[i], x_recv.at[i], {"fsdp": mate}))
    rest = [remote(own_ref.at[:, late], sketch.at[f, :, late], late_send.at[0, step], late_recv.at[0, step], line(step))
            for step in range(1, lines)]
    mates = [remote(sketch.at[mate, :, late], sketch.at[mate, :, late], late_send.at[1, step], late_recv.at[1, step], line(step))
             for step in range(1, lines)]
    blocks = n // BLOCK

    def ship(r):
        @pl.when(r == 0)
        def _():
            for copy in along + first:
                copy.start()

        @pl.when(r == 1)
        def _():
            own_copy.wait()
            for copy in rest:
                copy.start()
            first[0].wait_recv()
            for copy in mates:
                copy.start()
            for copy in along:
                copy.wait_recv()
            for copy in across:
                copy.start()

    def turn(r, carry):
        place = 0
        places = {}
        for i in range(blocks):
            strip = product(current[:, i * BLOCK:(i + 1) * BLOCK], current[:, i * BLOCK:], (0, 0))
            for j in range(i, blocks):
                packed[place:place + BLOCK, :] = strip[:, (j - i) * BLOCK:(j - i + 1) * BLOCK]
                places[i, j] = place
                place += BLOCK
        started = []
        source, base, size = packed, 0, place
        downs = ((land0, sum0, send0, recv0), (land1, sum1, send1, recv1), (land2, sum2, send2, recv2))
        for stage, (land, total_ref, send, recv) in zip(stages, downs):
            members, me, _ = stage
            size = size // members
            copies = exchange(stage, lambda i: source.at[rows(i, size)], lambda step: land.at[step], send, recv)
            started += copies
            total = source[rows(me, size), :]
            for step in range(1, members):
                copies[step - 1].wait_recv()
                total = total + land[step]
            total_ref[...] = total
            base = base + me * size
            source = total_ref
        gathered[pl.ds(pl.multiple_of(base, size), size), :] = total
        source = sum2
        for stage, (send, recv) in zip(stages[::-1], ((send3, recv3), (send4, recv4), (send5, recv5))):
            members, me, _ = stage
            spot = gathered.at[pl.ds(pl.multiple_of(base, size), size)]
            copies = exchange(stage, lambda i: source, lambda step: spot, send, recv)
            started += copies
            for copy in copies:
                copy.wait_recv()
            if members == count:
                ship(r)
            base = base - me * size
            size = size * members
            source = gathered.at[pl.ds(pl.multiple_of(base, size), size)]
        for copy in started:
            copy.wait_send()

        x_ref = inverses.at[r]
        for i in range(blocks):
            for j in range(i, blocks):
                x_ref[i * BLOCK:(i + 1) * BLOCK, j * BLOCK:(j + 1) * BLOCK] = gathered[places[i, j]:places[i, j] + BLOCK, :]
        inverse_kernel(x_ref, m_ref)
        current[...] = product(current[...], x_ref[...], (1, 1))
        return carry

    lax.fori_loop(0, 2, turn, 0)
    left_ref[...] = current[...]
    back_ref[...] = product(inverses[1], inverses[0], (1, 0))
    size = own_ref.shape[0]

    def multiply(side):
        def body(i, carry):
            turned_ref[:, rows(2 * i + side, size)] = product(back_ref[...], sketch[2 * i + side], (1, 1))
            return carry

        lax.fori_loop(0, lines, body, 0)

    for copy in rest:
        copy.wait_recv()
    multiply(x)
    for copy in across + mates:
        copy.wait_recv()
    multiply(1 - x)
    for copy in along + first + across + rest + mates:
        copy.wait_send()


def inverse_kernel(x_ref, m_ref):
    n = x_ref.shape[0]
    for start in range(0, n, BLOCK):
        stop = start + BLOCK
        m_ref[...] = x_ref[start:stop, start:stop]
        eliminate_block(m_ref)
        diagonal = m_ref[...]
        x_ref[start:stop, start:stop] = diagonal
        if start > 0:
            x_ref[start:stop, :start] = product(diagonal, x_ref[start:stop, :start], (1, 0))
        if stop < n:
            right = product(diagonal, x_ref[start:stop, stop:], (1, 0))
            if start > 0:
                x_ref[stop:, :start] -= product(right, x_ref[start:stop, :start], (0, 0))
            x_ref[stop:, start:stop] = -product(right, diagonal, (0, 0))
            x_ref[stop:, stop:] -= product(right, right, (0, 0))
            x_ref[start:stop, stop:] = jnp.zeros((BLOCK, n - stop), jnp.float32)


def orthonormal_chain(own, chips, count):
    rows, n = own.shape
    blocks = n // BLOCK
    packed = BLOCK * blocks * (blocks + 1) // 2
    dma = pltpu.SemaphoreType.DMA
    f32 = jnp.float32
    half, part = packed // 2, packed // 2 // chips
    return pl.pallas_call(
        functools.partial(chain_kernel, (chips, count)),
        out_shape=[jax.ShapeDtypeStruct((rows, n), f32), jax.ShapeDtypeStruct((n, rows * count), f32)],
        in_specs=[pl.BlockSpec(memory_space=pltpu.VMEM)],
        out_specs=[pl.BlockSpec(memory_space=pltpu.VMEM)] * 2,
        scratch_shapes=[
            pltpu.VMEM((rows, n), f32),
            pltpu.VMEM((2, n, n), f32),
            pltpu.VMEM((n, n), f32),
            pltpu.VMEM((count, rows, n), f32),
            pltpu.VMEM((packed, BLOCK), f32),
            pltpu.VMEM((packed, BLOCK), f32),
            pltpu.VMEM((2, half, BLOCK), f32),
            pltpu.VMEM((chips, part, BLOCK), f32),
            pltpu.VMEM((count, part // count, BLOCK), f32),
            pltpu.VMEM((half, BLOCK), f32),
            pltpu.VMEM((part, BLOCK), f32),
            pltpu.VMEM((part // count, BLOCK), f32),
            pltpu.VMEM((BLOCK, BLOCK), f32),
        ] + [dma((members,)) for members in (2, 2, chips, chips, count, count, count, count, chips, chips, 2, 2)]
        + [dma] + [dma((count // 2,))] * 4 + [dma((2, count // 2))] * 2,
        compiler_params=pltpu.CompilerParams(collective_id=2, has_side_effects=True, vmem_limit_bytes=40 * 1024 * 1024),
        cost_estimate=pl.CostEstimate(flops=2 * n * n * n * 40, bytes_accessed=16 * n * n, transcendentals=n),
        name="orthonormal_chain",
    )(own)


def inverse_factor(gram):
    n = gram.shape[0]

    def kernel(g_ref, x_ref, m_ref):
        x_ref[...] = g_ref[...]
        inverse_kernel(x_ref, m_ref)

    return pl.pallas_call(
        kernel,
        out_shape=jax.ShapeDtypeStruct((n, n), jnp.float32),
        in_specs=[pl.BlockSpec(memory_space=pltpu.VMEM)],
        out_specs=pl.BlockSpec(memory_space=pltpu.VMEM),
        scratch_shapes=[pltpu.VMEM((BLOCK, BLOCK), jnp.float32)],
        cost_estimate=pl.CostEstimate(flops=2 * n * n * n * 20, bytes_accessed=8 * n * n, transcendentals=n),
        name="inverse_factor",
    )(gram)


def pieces_of(value):
    high = value.astype(jnp.bfloat16)
    rest = value - high.astype(jnp.float32)
    middle = rest.astype(jnp.bfloat16)
    low = (rest - middle.astype(jnp.float32)).astype(jnp.bfloat16)
    return high, middle, low


def sketch_kernel(m_hbm, g_hbm, b_hbm, out_ref, m_buf, g_buf, land, split, part, land_x, summed, land_z,
                  m_sem, g_sem, own_sem, core_send, core_recv, y_send, y_recv, relay_send, relay_recv,
                  x_send, x_recv, z_send, z_recv):
    t, f = lax.axis_index("tp"), lax.axis_index("fsdp")
    y, c = t // 2, t % 2
    z, x = f // 2, f % 2
    width = b_hbm.shape[1]
    depth = m_hbm.shape[1]
    half = depth // 2
    block = m_hbm.shape[0] // 4
    own = block // 2
    core_peer = {"tp": 2 * y + 1 - c}
    y_peer = {"tp": 2 * (1 - y) + c}
    x_peer = {"fsdp": 2 * z + 1 - x}

    def order(j):
        return 2 * ((z // 2 + (3 - j) // 2) % 2) + (z % 2 + (3 - j) % 2) % 2

    barrier = pltpu.get_barrier_semaphore()
    for peer in [core_peer, y_peer, x_peer] + [{"fsdp": 2 * order(j) + x} for j in range(3)]:
        pl.semaphore_signal(barrier, inc=1, device_id=peer, device_id_type=MESH)

    def fetch(s):
        j = s % 4 * (s // 8) + (s // 2) * (1 - s // 8)
        k = (s % 2) * (1 - s // 8) + (s // 12)
        slot = s % 2
        rows = pl.ds(pl.multiple_of(order(j) * block, block), block)
        columns = pl.ds(pl.multiple_of(k * half, half), half)
        return (pltpu.make_async_copy(m_hbm.at[rows, columns], m_buf.at[slot], m_sem.at[slot]),
                pltpu.make_async_copy(g_hbm.at[rows, columns], g_buf.at[slot], g_sem.at[slot]))

    own_copy = pltpu.make_async_copy(b_hbm, land.at[0], own_sem)
    own_copy.start()
    for copy in fetch(0):
        copy.start()
    pl.semaphore_wait(barrier, 6)

    quarter = depth // 4

    def remote(source, target, send, recv, peer):
        return pltpu.make_async_remote_copy(src_ref=source, dst_ref=target, send_sem=send, recv_sem=recv,
                                            device_id=peer, device_id_type=MESH)

    to_core = [remote(b_hbm.at[pl.ds(k * half, half)], land.at[1, pl.ds(k * half, half)],
                      core_send.at[k], core_recv.at[k], core_peer) for k in range(2)]
    to_y = [remote(b_hbm.at[pl.ds(q * quarter, quarter)], land.at[2, pl.ds(q * quarter, quarter)],
                   y_send.at[q], y_recv.at[q], y_peer) for q in range(4)]
    relay = [remote(land.at[2, pl.ds(q * quarter, quarter)], land.at[3, pl.ds(q * quarter, quarter)],
                    relay_send.at[q], relay_recv.at[q], core_peer) for q in range(4)]
    for copy in to_core + to_y:
        copy.start()

    def cut(slot, column, k):
        columns = pl.ds(pl.multiple_of(column * width, width), width)

        def body(i, carry):
            rows = pl.ds(pl.multiple_of(k * half + i * CHUNK, CHUNK), CHUNK)
            high, middle, low = pieces_of(land[slot, rows, :])
            for place, piece in enumerate((high, middle, low, high, middle, high)):
                split[k, i, place * CHUNK:(place + 1) * CHUNK, columns] = piece
            return carry

        lax.fori_loop(0, half // CHUNK, body, 0)

    part[...] = jnp.zeros_like(part)
    own_copy.wait()
    cut(0, c, 0)
    to_core[0].wait_recv()
    cut(1, 1 - c, 0)

    across = [[remote(part.at[n, j, pl.ds(pl.multiple_of((1 - x) * own, own), own)], land_x.at[n, j],
                      x_send.at[n, j], x_recv.at[n, j], x_peer) for j in range(4)] for n in range(2)]
    along = [[remote(summed.at[n, j], land_z.at[n, j], z_send.at[n, j], z_recv.at[n, j],
                     {"fsdp": 2 * order(j) + x}) for j in range(3)] for n in range(2)]

    def add_x(n, j):
        across[n][j].wait_recv()

        def body(i, carry):
            rows = pl.ds(pl.multiple_of(i * 64, 64), 64)
            mine = pl.ds(pl.multiple_of(x * own + i * 64, 64), 64)
            summed[n, j, rows, :] = part[n, j, mine, :] + land_x[n, j, rows, :]
            return carry

        lax.fori_loop(0, own // 64, body, 0)
        if j < 3:
            along[n][j].start()

    before = {}
    after = {}

    def at(table, s, action):
        table.setdefault(s, []).append(action)

    def second_half():
        cut(0, c, 1)
        to_core[1].wait_recv()
        cut(1, 1 - c, 1)

    def pass_on(q):
        to_y[q].wait_recv()
        relay[q].start()

    def other_chip(k):
        cut(2, c, k)
        relay[2 * k].wait_recv()
        relay[2 * k + 1].wait_recv()
        cut(3, 1 - c, k)

    at(before, 1, second_half)
    at(before, 4, lambda: pass_on(0))
    at(before, 7, lambda: pass_on(1))
    at(before, 8, lambda: other_chip(0))
    at(before, 10, lambda: pass_on(2))
    at(before, 12, lambda: pass_on(3))
    at(before, 12, lambda: other_chip(1))
    for j in range(4):
        at(after, 2 * j + 1, lambda j=j: across[0][j].start())
        at(after, 2 * j + 3, lambda j=j: add_x(0, j))
        at(after, 12 + j, lambda j=j: across[1][j].start())
    at(after, 14, lambda: add_x(1, 0))
    at(after, 15, lambda: add_x(1, 1))

    def step(s, carry):
        for copy in fetch(s):
            copy.wait()

        @pl.when(s < 15)
        def _():
            for copy in fetch(s + 1):
                copy.start()

        for when, actions in before.items():
            @pl.when(s == when)
            def _(actions=actions):
                for action in actions:
                    action()

        slot = s % 2
        j = s % 4 * (s // 8) + (s // 2) * (1 - s // 8)
        k = (s % 2) * (1 - s // 8) + (s // 12)
        n = s // 8

        def body(i, inner):
            columns = pl.ds(pl.multiple_of(i * CHUNK, CHUNK), CHUNK)
            value = m_buf[slot, :, columns] + g_buf[slot, :, columns].astype(jnp.float32)
            high, middle, low = pieces_of(value)
            left = jnp.concatenate([high, high, high, middle, middle, low], axis=1)
            part[n, j] += jnp.dot(left, split[k, i], preferred_element_type=jnp.float32)
            return inner

        lax.fori_loop(0, half // CHUNK, body, 0, unroll=True)
        for when, actions in after.items():
            @pl.when(s == when)
            def _(actions=actions):
                for action in actions:
                    action()
        return carry

    lax.fori_loop(0, 16, step, 0)
    add_x(1, 2)
    add_x(1, 3)
    for n in range(2):
        for j in range(3):
            along[n][j].wait_recv()
        columns = pl.ds(pl.multiple_of((y * (1 - n) + (1 - y) * n) * 2 * width, 2 * width), 2 * width)
        out_ref[:, columns] = summed[n, 3] + land_z[n, 0] + land_z[n, 1] + land_z[n, 2]
    for copy in to_core + to_y + relay + across[0] + across[1] + along[0] + along[1]:
        copy.wait_send()


def sketch_rows(momentum, gradient, basis):
    rows, depth = momentum.shape
    width = basis.shape[1]
    block, half = rows // 4, depth // 2
    own = block // 2
    dma = pltpu.SemaphoreType.DMA
    f32 = jnp.float32
    return pl.pallas_call(
        sketch_kernel,
        out_shape=jax.ShapeDtypeStruct((own, 4 * width), f32),
        in_specs=[pl.BlockSpec(memory_space=pl.ANY)] * 3,
        out_specs=pl.BlockSpec(memory_space=pltpu.VMEM),
        scratch_shapes=[
            pltpu.VMEM((2, block, half), f32),
            pltpu.VMEM((2, block, half), jnp.bfloat16),
            pltpu.VMEM((4, depth, width), f32),
            pltpu.VMEM((2, half // CHUNK, 6 * CHUNK, 2 * width), jnp.bfloat16),
            pltpu.VMEM((2, 4, block, 2 * width), f32),
            pltpu.VMEM((2, 4, own, 2 * width), f32),
            pltpu.VMEM((2, 4, own, 2 * width), f32),
            pltpu.VMEM((2, 3, own, 2 * width), f32),
            dma((2,)), dma((2,)), dma, dma((2,)), dma((2,)), dma((4,)), dma((4,)), dma((4,)), dma((4,)),
            dma((2, 4)), dma((2, 4)), dma((2, 3)), dma((2, 3)),
        ],
        compiler_params=pltpu.CompilerParams(collective_id=1, has_side_effects=True, vmem_limit_bytes=60 * 1024 * 1024),
        cost_estimate=pl.CostEstimate(flops=12 * rows * depth * 4 * width, bytes_accessed=12 * rows * depth, transcendentals=0),
        name="sketch_rows",
    )(momentum, gradient, basis)


def right_kernel(count, m_hbm, g_hbm, left_ref, right_ref, basis_ref, m_buf, g_buf, high_ref, low_ref, part, land_c, summed, land_y,
                 rows_ref, squares, land_s, m_sem, g_sem, core_send, core_recv, y_send, y_recv, keep_send, keep_recv,
                 over_send, over_recv, relay_send, relay_recv, s_send, s_recv):
    t, f = lax.axis_index("tp"), lax.axis_index("fsdp")
    y, c = t // 2, t % 2
    rank, depth = left_ref.shape
    width = rank // 4
    steps = part.shape[0]
    core_peer = {"tp": 2 * y + 1 - c}
    y_peer = {"tp": 2 * (1 - y) + c}
    other = 2 * (1 - y) + c

    barrier = pltpu.get_barrier_semaphore()
    for peer in [core_peer, y_peer] + [{"fsdp": lax.rem(f + step, count)} for step in range(1, count)]:
        pl.semaphore_signal(barrier, inc=1, device_id=peer, device_id_type=MESH)

    def fetch(s):
        columns = pl.ds(pl.multiple_of(s * CHUNK, CHUNK), CHUNK)
        return (pltpu.make_async_copy(m_hbm.at[:, columns], m_buf.at[s % 2], m_sem.at[s % 2]),
                pltpu.make_async_copy(g_hbm.at[:, columns], g_buf.at[s % 2], g_sem.at[s % 2]))

    for copy in fetch(0):
        copy.start()

    def remote(source, target, send, recv, peer):
        return pltpu.make_async_remote_copy(src_ref=source, dst_ref=target, send_sem=send, recv_sem=recv,
                                            device_id=peer, device_id_type=MESH)

    def band(index):
        return pl.ds(pl.multiple_of(index * width, width), width)

    def spot(index, s):
        return right_ref.at[band(index), pl.ds(pl.multiple_of(s * CHUNK, CHUNK), CHUNK)]

    def to_core(s, chip):
        return remote(part.at[s, band(2 * chip + 1 - c)], land_c.at[s, chip], core_send.at[s, chip], core_recv.at[s, chip], core_peer)

    def to_y(s):
        return remote(summed.at[s, 1 - y], land_y.at[s], y_send.at[s], y_recv.at[s], y_peer)

    def keep(s):
        return remote(spot(t, s), spot(t, s), keep_send.at[s], keep_recv.at[s], core_peer)

    def over(s):
        return remote(spot(t, s), spot(t, s), over_send.at[s], over_recv.at[s], y_peer)

    def relay(s):
        return remote(spot(other, s), spot(other, s), relay_send.at[s], relay_recv.at[s], core_peer)

    def split(i, carry):
        columns = pl.ds(pl.multiple_of(i * CHUNK, CHUNK), CHUNK)
        value = left_ref[:, columns]
        high = value.astype(jnp.bfloat16)
        high_ref[i] = high
        low_ref[i] = (value - high.astype(jnp.float32)).astype(jnp.bfloat16)
        return carry

    lax.fori_loop(0, depth // CHUNK, split, 0)
    squares[...] = jnp.zeros_like(squares)
    pl.semaphore_wait(barrier, 1 + count)

    def step(s, carry):
        @pl.when(s < steps)
        def _():
            for copy in fetch(s):
                copy.wait()

            @pl.when(s < steps - 1)
            def _():
                for copy in fetch(s + 1):
                    copy.start()

            part[s] = jnp.zeros((rank, CHUNK), jnp.float32)

            def body(i, inner):
                rows = pl.ds(pl.multiple_of(i * CHUNK, CHUNK), CHUNK)
                value = m_buf[s % 2, rows, :] + g_buf[s % 2, rows, :].astype(jnp.float32)
                high = value.astype(jnp.bfloat16)
                low = (value - high.astype(jnp.float32)).astype(jnp.bfloat16)
                left = jnp.concatenate([high_ref[i], high_ref[i], low_ref[i]], axis=1)
                part[s] += jnp.dot(left, jnp.concatenate([high, low, high], axis=0), preferred_element_type=jnp.float32)
                return inner

            lax.fori_loop(0, depth // CHUNK, body, 0, unroll=True)
            for chip in range(2):
                to_core(s, chip).start()

        @pl.when((s >= 1) & (s < steps + 1))
        def _():
            now = s - 1
            for chip in range(2):
                to_core(now, chip).wait_recv()
                summed[now, chip] = part[now, band(2 * chip + c), :] + land_c[now, chip]
            to_y(now).start()

        @pl.when((s >= 4) & (s < steps + 4))
        def _():
            now = s - 4
            to_y(now).wait_recv()
            mine = summed[now, y] + land_y[now]
            right_ref[band(t), pl.ds(pl.multiple_of(now * CHUNK, CHUNK), CHUNK)] = mine
            over(now).start()
            keep(now).start()
            turned = mine.T
            rows_ref[pl.ds(pl.multiple_of(now * CHUNK, CHUNK), CHUNK), :] = turned
            squares[...] += jnp.sum((turned * turned).reshape(CHUNK // 8, 8, width), axis=0)

        @pl.when(s >= 7)
        def _():
            now = s - 7
            over(now).wait_recv()
            relay(now).start()
        return carry

    lax.fori_loop(0, steps + 4, step, 0)
    spread = [remote(squares, land_s.at[step], s_send.at[step], s_recv.at[step], {"fsdp": lax.rem(f + step, count)})
              for step in range(1, count)]
    for copy in spread:
        copy.start()
    total = squares[...]
    for step in range(1, count):
        spread[step - 1].wait_recv()
        total = total + land_s[step]
    scale = jnp.sqrt(jnp.sum(total, axis=0, keepdims=True) + tiny)

    def divide(i, carry):
        rows = pl.ds(pl.multiple_of(i * CHUNK, CHUNK), CHUNK)
        basis_ref[rows, :] = rows_ref[rows, :] / scale
        return carry

    lax.fori_loop(0, steps, divide, 0)

    def last(s, carry):
        over(s).wait_recv()
        relay(s).start()
        return carry

    lax.fori_loop(steps - 3, steps, last, 0)

    def drain(s, carry):
        for chip in range(2):
            to_core(s, chip).wait_send()
        to_y(s).wait_send()
        over(s).wait_send()
        keep(s).wait()
        relay(s).wait()
        return carry

    lax.fori_loop(0, steps, drain, 0)
    for copy in spread:
        copy.wait_send()


def right_columns(momentum, gradient, left, count):
    rows, depth = momentum.shape
    rank = left.shape[0]
    width = rank // 4
    steps = depth // CHUNK
    dma = pltpu.SemaphoreType.DMA
    f32 = jnp.float32
    return pl.pallas_call(
        functools.partial(right_kernel, count),
        out_shape=[jax.ShapeDtypeStruct((rank, depth), f32), jax.ShapeDtypeStruct((depth, width), f32)],
        in_specs=[pl.BlockSpec(memory_space=pl.ANY)] * 2 + [pl.BlockSpec(memory_space=pltpu.VMEM)],
        out_specs=[pl.BlockSpec(memory_space=pltpu.VMEM)] * 2,
        scratch_shapes=[
            pltpu.VMEM((2, rows, CHUNK), f32),
            pltpu.VMEM((2, rows, CHUNK), jnp.bfloat16),
            pltpu.VMEM((rows // CHUNK, rank, CHUNK), jnp.bfloat16),
            pltpu.VMEM((rows // CHUNK, rank, CHUNK), jnp.bfloat16),
            pltpu.VMEM((steps, rank, CHUNK), f32),
            pltpu.VMEM((steps, 2, width, CHUNK), f32),
            pltpu.VMEM((steps, 2, width, CHUNK), f32),
            pltpu.VMEM((steps, width, CHUNK), f32),
            pltpu.VMEM((depth, width), f32),
            pltpu.VMEM((8, width), f32),
            pltpu.VMEM((count, 8, width), f32),
            dma((2,)), dma((2,)), dma((steps, 2)), dma((steps, 2)), dma((steps,)), dma((steps,)), dma((steps,)), dma((steps,)),
            dma((steps,)), dma((steps,)), dma((steps,)), dma((steps,)), dma((count,)), dma((count,)),
        ],
        compiler_params=pltpu.CompilerParams(collective_id=3, has_side_effects=True, vmem_limit_bytes=60 * 1024 * 1024),
        cost_estimate=pl.CostEstimate(flops=6 * rows * depth * rank, bytes_accessed=6 * rows * depth, transcendentals=0),
        name="right_columns",
    )(momentum, gradient, left)


def sketch_own(momentum, gradient, basis, fitting):
    if fitting:
        return sketch_rows(momentum, gradient, basis)
    tile = momentum + gradient.astype(jnp.float32)
    partial_sketch = product(tile, lax.all_gather(basis, "tp", axis=1, tiled=True), (1, 0))
    return lax.psum_scatter(partial_sketch, "fsdp", scatter_dimension=0, tiled=True)


def orthonormal(own):
    inverse = inverse_factor(lax.psum(product(own, own, (0, 0)), ("fsdp", "tp")))
    return product(own, inverse, (1, 1)), inverse


def on_device(momentum, gradient, basis):
    fitting = lax.axis_size("tp") == 4 and lax.axis_size("fsdp") == 8
    own = sketch_own(momentum, gradient, basis, fitting)
    if fitting:
        own_left, left = orthonormal_chain(own, lax.axis_size("tp") // 2, lax.axis_size("fsdp"))
        right, new_basis = right_columns(momentum, gradient, left, lax.axis_size("fsdp"))
        change = product(left, (1.0 - keep_rate) * right, (0, 0), lax.Precision.DEFAULT)
        return (momentum + gradient.astype(jnp.float32) - change, new_basis, own_left)
    tile = momentum + gradient.astype(jnp.float32)
    sketch = lax.all_gather(own, "fsdp", axis=0, tiled=True)
    own_first, inverse = orthonormal(own)
    own_left, second = orthonormal(own_first)
    left = product(sketch, product(second, inverse, (1, 0)), (1, 1))
    partial_right = product(tile, left, (0, 0), lax.Precision.HIGH)
    mine = lax.psum_scatter(partial_right, "tp", scatter_dimension=1, tiled=True)
    squares = lax.psum(jnp.sum(mine * mine, axis=0), "fsdp")
    new_basis = mine / jnp.sqrt(squares + tiny)[None, :]
    full_right = lax.all_gather(mine, "tp", axis=1, tiled=True)
    new_momentum = tile - product(left, (1.0 - keep_rate) * full_right, (1, 1), lax.Precision.DEFAULT)
    return (new_momentum, new_basis, own_left)


def solution(mesh):
    placed = (P("tp", "fsdp"), P("tp", "fsdp"), P("fsdp", "tp"))
    return jax.shard_map(
        on_device,
        mesh=mesh,
        in_specs=placed,
        out_specs=(P("tp", "fsdp"), P("fsdp", "tp"), P(("tp", "fsdp"), None)),
        check_vma=False,
    )
```
